512 devices in a mesh: seq: 64 (over z, y), tp: 8 (over x, core).
Axes of the slice: x: 4, y: 4, z: 16, core: 2. Of those that a mesh axis runs over, the one named last changes fastest.
Arguments:
- residual: bfloat16 [8192, 8192], P('seq', 'tp'), may hold values from -6 to 6
- steer_table: bfloat16 [7, 8192], P(None, 'tp'), may hold values from -6 to 6
- steer_index: int32 [4], replicated, may hold values from 0 to 6
- steer_num: int32 [4], replicated, may hold values from -8 to 8
- lengths: int32 [4], replicated, may hold values from 1 to 4096, 8192 in all
- queries: bfloat16 [8192, 64, 128], P('seq', 'tp'), may hold values from -128 to 128
- keys: bfloat16 [8192, 8, 128], P('seq', 'tp'), may hold values from -6 to 6
- values: bfloat16 [8192, 8, 128], P('seq', 'tp'), may hold values from -6 to 6
- inner_x: bfloat16 [8192, 16384], P('seq', 'tp'), may hold values from -6 to 6
- dt_raw: bfloat16 [8192, 16384], P('seq', 'tp'), may hold values from -4 to 4
- dt_bias: float32 [16384], P('tp'), may hold values from -7 to -2.5
- a_log: float32 [16, 16384], P(None, 'tp'), may hold values from -2.3 to 2.77
- skip_gain: float32 [16384], P('tp'), may hold values from 0.5 to 1.5
- bc_weight: bfloat16 [32, 16384], P(None, 'tp'), may hold values from -0.046875 to 0.046875
Outputs:
- steered: bfloat16 [8192, 8192], P('seq', 'tp')
- context: bfloat16 [8192, 64, 128], P('seq', 'tp')
- mixed: bfloat16 [8192, 16384], P('seq', 'tp')
The draws below stay inside these ranges and needn't reach their ends.
Inputs may be any that keep to these rules, and one draw needn't show every extreme that they name: `lengths`: the 4 requests lie end to end in token order and the longest has exactly 8192 // 2 tokens. `steer_num`: a request's steering multiplier is its numerator over 4.
All inputs are finite; a program needn't handle non-finite values.
Results may differ from the reference program's by a relative error of at most 0.0039.
Values may be sent and summed in bfloat16 or wider, within the bound.
A program may use at most 128 MiB of HBM per device.

```python
import math
import jax
import jax.numpy as jnp
import numpy as np
from jax import lax

D = 8192
KV_HEADS = 8
HEAD_DIM = 128
CHANNELS = 16384
STATE = 16
Q_HEADS = 64
NVEC = 7
REQS = 4
TOKENS = 8192


def shared_keys(key):
    base = jax.random.normal(jax.random.fold_in(key, 11), (TOKENS, KV_HEADS, HEAD_DIM), jnp.float32)
    return jnp.clip(base, -6.0, 6.0)


def draw_keys(key, part):
    base = shared_keys(key)
    return base.astype(jnp.bfloat16)


def draw_queries(key, part):
    drawn = 3.0 * jnp.clip(jax.random.normal(jax.random.fold_in(key, 12), (TOKENS, Q_HEADS, HEAD_DIM), jnp.float32), -6.0, 6.0)
    return drawn.astype(jnp.bfloat16)


def with_ends(drawn, stream_key, least, top_value):
    longest = drawn.shape.index(max(drawn.shape))
    spots = []
    for shift in (0, 1):
        where = [jax.random.randint(jax.random.fold_in(stream_key, axis), (), 0, length) for axis, length in enumerate(drawn.shape)]
        where[longest] = (where[longest] + shift) % drawn.shape[longest]
        spots.append(tuple(where))
    return drawn.at[spots[0]].set(least).at[spots[1]].set(top_value)


def shard_levels(rng, dims, cuts, least, largest):
    def one(axis_at, blocks):
        steps = jax.random.uniform(jax.random.fold_in(jax.random.fold_in(rng, 6), axis_at), (blocks,), jnp.float32, least / len(cuts), largest / len(cuts))
        return jnp.repeat(jnp.exp(steps), dims[axis_at] // blocks).reshape((-1,) + (1,) * (len(dims) - axis_at - 1))

    factor_of = one(*cuts[0])
    for cut in cuts[1:]:
        factor_of = factor_of * one(*cut)
    return factor_of


def length_profile(count, total, reach, slope):
    portions = [(1 << 20) // math.isqrt(standing ** slope) + 1 for standing in range(2, count + 1)]
    rest, holding = total - reach - (count - 1), [1] * (count - 1)
    while rest > 0:
        free = [i for i in range(count - 1) if holding[i] < reach]
        pool, remaining = sum([portions[i] for i in free]), rest
        for i in free:
            more = min(reach - holding[i], max(1, remaining * portions[i] // pool), rest)
            holding[i] = holding[i] + more
            rest = rest - more
    return np.array([reach] + holding)


def uneven_parts(stream_key, number_of, total, most, slope):
    if number_of == 2:
        one = jax.random.randint(stream_key, (), max(1, total - most), min(most, total - 1) + 1)
        return jnp.stack([one, total - one])
    sizes = jnp.asarray(length_profile(number_of, total, most, slope), jnp.int32)
    twos = (number_of - 1) // 2
    giver, receiver = sizes[1:1 + 2 * twos:2], sizes[2:2 + 2 * twos:2]
    margin = jnp.minimum(giver - 1, most - receiver)
    passed = jax.random.randint(jax.random.fold_in(stream_key, 1), (twos,), 0, 1 << 20) % (margin + 1)
    sizes = sizes.at[1:1 + 2 * twos:2].set(giver - passed).at[2:2 + 2 * twos:2].set(receiver + passed)
    return sizes[jax.random.permutation(jax.random.fold_in(stream_key, 2), number_of)]


def normal_values(own_key, shape, width, most, shards=(), kind=jnp.bfloat16):
    drawn = jax.random.normal(own_key, shape, jnp.float32) * width
    if len(shards) > 0:
        drawn = shard_levels(own_key, shape, shards, -0.22, 0.18) * drawn
    return jnp.clip(drawn, min=-most, max=most).astype(kind)


def setup_inputs(seed: int = 0) -> dict:
    key_list = jax.random.split(jax.random.key(seed), 15)
    residual = normal_values(key_list[0], (TOKENS, D), 1.0, 6.0, ((0, 64), (1, 8)))
    steer_table = normal_values(key_list[1], (NVEC, D), 1.0, 6.0, ((1, 8),))
    steer_index = with_ends(jax.random.randint(key_list[2], (REQS,), 0, NVEC), jax.random.fold_in(key_list[2], 1), 0, NVEC - 1).astype(jnp.int32)
    steer_num = with_ends(jax.random.randint(key_list[3], (REQS,), -8, 9), jax.random.fold_in(key_list[3], 1), -8, 8).astype(jnp.int32)
    lengths = uneven_parts(key_list[4], REQS, TOKENS, TOKENS // 2, 2).astype(jnp.int32)
    queries = draw_queries(jax.random.fold_in(key_list[14], 71), 0)
    keys = draw_keys(jax.random.fold_in(key_list[14], 71), 0)
    values = normal_values(key_list[7], (TOKENS, KV_HEADS, HEAD_DIM), 1.0, 6.0, ((0, 64), (1, 8)))
    inner_x = normal_values(key_list[8], (TOKENS, CHANNELS), 1.0, 6.0, ((0, 64), (1, 8)))
    dt_raw = normal_values(key_list[9], (TOKENS, CHANNELS), 1.0, 4.0, ((0, 64), (1, 8)))
    dt_bias = jnp.clip(-7.0 + 4.5 * jax.random.uniform(key_list[10], (CHANNELS,), jnp.float32) ** shard_levels(key_list[10], (CHANNELS,), ((0, 8),), -0.2, 0.2), -7.0, -2.5)
    a_log = jnp.clip(-2.3 + 5.0699999 * jax.random.uniform(key_list[11], (STATE, CHANNELS), jnp.float32) ** shard_levels(key_list[11], (STATE, CHANNELS), ((1, 8),), -0.2, 0.2), -2.3, 2.77)
    skip_gain = jnp.clip(1.0 + 0.1 * jax.random.normal(key_list[12], (CHANNELS,), jnp.float32), 0.5, 1.5)
    bc_weight = normal_values(key_list[13], (2 * STATE, CHANNELS), CHANNELS ** -0.5, 0.046875, ((1, 8),))
    return dict(residual=residual, steer_table=steer_table, steer_index=steer_index, steer_num=steer_num, lengths=lengths, queries=queries, keys=keys, values=values, inner_x=inner_x, dt_raw=dt_raw, dt_bias=dt_bias, a_log=a_log, skip_gain=skip_gain, bc_weight=bc_weight)


NEG_FILL = -1e30


def request_bounds(lengths, positions):
    seg_ends = jnp.cumsum(lengths).astype(jnp.int32)
    seg_starts = (seg_ends - lengths).astype(jnp.int32)
    member = (positions[:, None] >= seg_starts[None, :]) & (positions[:, None] < seg_ends[None, :])
    member_int = member.astype(jnp.int32)
    req_start = jnp.sum(member_int * seg_starts[None, :], axis=1).astype(jnp.int32)
    return member_int, req_start


def reference(residual, steer_table, steer_index, steer_num, lengths, queries, keys, values, inner_x, dt_raw, dt_bias, a_log, skip_gain, bc_weight):
    positions = jnp.arange(TOKENS, dtype=jnp.int32)
    member_int, req_start = request_bounds(lengths, positions)
    request_id = jnp.sum(member_int * jnp.arange(REQS, dtype=jnp.int32)[None, :], axis=1).astype(jnp.int32)
    per_request = steer_table.astype(jnp.float32)[steer_index] * (steer_num.astype(jnp.float32) * 0.25)[:, None]
    steered = (residual.astype(jnp.float32) + per_request[request_id]).astype(jnp.bfloat16)

    head_group = Q_HEADS // KV_HEADS
    score_scale = 1.0 / (HEAD_DIM ** 0.5)
    query_block = 64
    key_float = keys.astype(jnp.float32)
    value_float = values.astype(jnp.float32)
    query_blocks = queries.reshape(TOKENS // query_block, query_block, KV_HEADS, head_group, HEAD_DIM)
    pos_blocks = positions.reshape(TOKENS // query_block, query_block)
    start_blocks = req_start.reshape(TOKENS // query_block, query_block)
    key_pos = jnp.arange(TOKENS, dtype=jnp.int32)

    def attend(item):
        query_part, pos_part, start_part = item
        scores = jnp.einsum("tkgd,skd->tkgs", query_part.astype(jnp.float32), key_float) * score_scale
        allowed = (key_pos[None, :] <= pos_part[:, None]) & (key_pos[None, :] >= start_part[:, None])
        allowed = allowed[:, None, None, :]
        masked = jnp.where(allowed, scores, NEG_FILL)
        top_score = jnp.max(masked, axis=-1, keepdims=True)
        expo = jnp.where(allowed, jnp.exp(masked - top_score), 0.0)
        weights = expo.astype(jnp.bfloat16).astype(jnp.float32)
        numer = jnp.einsum("tkgs,skd->tkgd", weights, value_float)
        denom = jnp.sum(expo, axis=-1)
        return (numer / denom[..., None]).astype(jnp.bfloat16)

    context = lax.map(attend, (query_blocks, pos_blocks, start_blocks)).reshape(TOKENS, Q_HEADS, HEAD_DIM)

    mixed_bc = jnp.dot(inner_x, bc_weight.T, preferred_element_type=jnp.float32)
    b_rows = mixed_bc[:, :STATE]
    c_rows = mixed_bc[:, STATE:]
    keep_rows = jnp.where(positions == req_start, 0.0, 1.0).astype(jnp.float32)
    rates = jnp.exp(a_log)

    def token_step(state, item):
        raw_row, x_row, b_row, c_row, keep_row = item
        step_size = jax.nn.softplus(raw_row.astype(jnp.float32) + dt_bias)
        x_float = x_row.astype(jnp.float32)
        factor = jnp.exp(-step_size[None, :] * rates) * keep_row
        state = factor * state + (step_size * x_float)[None, :] * b_row[:, None]
        out_row = jnp.sum(c_row[:, None] * state, axis=0) + skip_gain * x_float
        return state, out_row.astype(jnp.bfloat16)

    _, mixed = lax.scan(token_step, jnp.zeros((STATE, CHANNELS), jnp.float32), (dt_raw, inner_x, b_rows, c_rows, keep_rows))
    return steered, context, mixed
```

```python
import functools
import jax
import jax.numpy as jnp
from jax import lax
from jax.experimental import pallas as pl
from jax.experimental.pallas import tpu as pltpu
from jax.sharding import PartitionSpec as P

LOG2E = 1.4426950408889634
NEG_FILL = -1e30
RESET = 1e30
YN = 4
ZN = 16
SEQ = YN * ZN
TPN = 8
WIN = 8
TOK = 128
GROUP = 16
MESH = pl.DeviceIdType.MESH
F32 = jnp.float32
BF16 = jnp.bfloat16


def gather_kernel(kv_ref, x_ref, w_ref, win_ref, bc_ref, parts, own_sem, zs, zr, rs, rr, ls, lr, ks, kr, vs, vr, bs, br):
    seq = lax.axis_index("seq")
    tp = lax.axis_index("tp")
    z = seq // YN
    y = lax.rem(seq, YN)
    left_y = lax.rem(y + YN - 1, YN)
    right_y = lax.rem(y + 1, YN)
    up = lax.rem(z + 1, ZN) * YN + y
    down = lax.rem(z + ZN - 1, ZN) * YN + y
    right = z * YN + right_y
    left = z * YN + left_y
    far_y = lax.rem(y + 2, YN)

    barrier = pltpu.get_barrier_semaphore()
    for peer in (up, down, right, left):
        pl.semaphore_signal(barrier, inc=1, device_id=(peer, tp), device_id_type=MESH)
    for off in range(1, TPN):
        pl.semaphore_signal(barrier, inc=1, device_id=(seq, lax.rem(tp + off, TPN)), device_id_type=MESH)
    pl.semaphore_wait(barrier, 4 + TPN - 1)

    def remote(src, dst, ssem, rsem, peer):
        return pltpu.make_async_remote_copy(
            src_ref=src, dst_ref=dst, send_sem=ssem, recv_sem=rsem, device_id=(peer, tp), device_id_type=MESH
        )

    def block(s):
        return kv_ref if s == 0 else win_ref.at[s, y]

    def z_copy(s):
        return remote(block(s - 1), win_ref.at[s, y], zs.at[s], zr.at[s], up)

    def right_copy(s):
        return remote(block(s), win_ref.at[s, y], rs.at[s], rr.at[s], right)

    def left_copy(s):
        return remote(block(s), win_ref.at[s, y], ls.at[s], lr.at[s], left)

    def k_copy(s):
        return remote(win_ref.at[s, left_y, 0], win_ref.at[s, left_y, 0], ks.at[s], kr.at[s], right)

    def v_copy(s):
        return remote(win_ref.at[s, right_y, 1], win_ref.at[s, right_y, 1], vs.at[s], vr.at[s], left)

    own = pltpu.make_async_copy(kv_ref, win_ref.at[0, y], own_sem)
    z_copy(1).start()
    right_copy(0).start()
    left_copy(0).start()
    own.start()

    parts[tp] = lax.dot_general(w_ref[...], x_ref[...], (((1,), (1,)), ((), ())), preferred_element_type=F32)

    def bc_copy(off):
        return pltpu.make_async_remote_copy(
            src_ref=parts.at[tp], dst_ref=parts.at[tp], send_sem=bs.at[off], recv_sem=br.at[off],
            device_id=(seq, lax.rem(tp + off, TPN)), device_id_type=MESH,
        )

    for off in range(1, TPN):
        bc_copy(off).start()

    for s in range(1, WIN + 1):
        z_copy(s).wait_recv()
        if s < WIN:
            z_copy(s + 1).start()
        right_copy(s).start()
        left_copy(s).start()
        right_copy(s - 1).wait_recv()
        k_copy(s - 1).start()
        left_copy(s - 1).wait_recv()
        v_copy(s - 1).start()
    right_copy(WIN).wait_recv()
    k_copy(WIN).start()
    left_copy(WIN).wait_recv()
    v_copy(WIN).start()
    for off in range(1, TPN):
        bc_copy(off).wait()
    total = parts[0]
    for t in range(1, TPN):
        total = total + parts[t]
    bc_ref[...] = total
    own.wait()
    for s in range(WIN + 1):
        if s > 0:
            z_copy(s).wait_send()
        right_copy(s).wait_send()
        left_copy(s).wait_send()
        k_copy(s).wait()
        v_copy(s).wait()


def gather(kv, x, w):
    vm = pl.BlockSpec(memory_space=pltpu.VMEM)
    dma = pltpu.SemaphoreType.DMA
    n = WIN + 1
    return pl.pallas_call(
        gather_kernel,
        out_shape=(
            jax.ShapeDtypeStruct((n, YN, 2, TOK, 128), BF16),
            jax.ShapeDtypeStruct((32, TOK), F32),
        ),
        in_specs=[vm, vm, vm],
        out_specs=(pl.BlockSpec(memory_space=pl.ANY), vm),
        scratch_shapes=[pltpu.VMEM((TPN, 32, TOK), F32), dma(())] + [dma((n,)) for _ in range(10)] + [dma((TPN,)), dma((TPN,))],
        compiler_params=pltpu.CompilerParams(collective_id=0, has_side_effects=True),
        name="gather_kv_bc",
    )(kv, x, w)


def log1p_exp(v):
    return jnp.maximum(v, 0.0) + jnp.log1p(jnp.exp(-jnp.abs(v)))


def fill_group(g, dt_ref, x_ref, bias, rates_unused, keep_ref, step_s, u_s):
    rows = pl.ds(pl.multiple_of(g * GROUP, GROUP), GROUP)
    raw = dt_ref[rows, :].astype(F32)
    x = x_ref[rows, :].astype(F32)
    step = log1p_exp(raw + bias)
    u_s[...] = (step * x).reshape(GROUP, 16, 128)
    step_s[...] = (step + keep_ref[rows, 0:1]).reshape(GROUP, 16, 128)
    return x


def local_kernel(bc_ref, dt_ref, x_ref, bias_ref, alog_ref, add_ref, tile_ref, rate_s, step_s, u_s, state_s, sum_s):
    rate_s[...] = (jnp.exp(alog_ref[...]) * (-LOG2E)).reshape(16, 16, 128)
    state_s[...] = jnp.zeros_like(state_s)
    sum_s[...] = jnp.zeros_like(sum_s)
    bias = bias_ref[...]

    @pl.loop(0, TOK // GROUP)
    def _(g):
        fill_group(g, dt_ref, x_ref, bias, None, add_ref, step_s, u_s)

        def token(t, carry):
            states, total = carry
            st = step_s[t]
            u = u_s[t]
            p = g * GROUP + t
            new = []
            for n in range(16):
                f = jnp.exp2(st * rate_s[n])
                new.append(f * states[n] + u * bc_ref[n, p])
            return tuple(new), total + st

        states, total = lax.fori_loop(0, GROUP, token, (tuple(state_s[n] for n in range(16)), sum_s[...]))
        for n in range(16):
            state_s[n] = states[n]
        sum_s[...] = total

    total = sum_s[...]
    for n in range(16):
        s = state_s[n]
        for q in range(4):
            tile_ref[n * 4 + q, 0:4, :] = s[4 * q : 4 * q + 4]
            tile_ref[n * 4 + q, 4:8, :] = total[4 * q : 4 * q + 4]


def local_pass(bc, dt, x, bias, a_log, reset_add):
    vm = pl.BlockSpec(memory_space=pltpu.VMEM)
    sm = pl.BlockSpec(memory_space=pltpu.SMEM)
    return pl.pallas_call(
        local_kernel,
        out_shape=jax.ShapeDtypeStruct((SEQ, 8, 128), F32),
        in_specs=[sm, vm, vm, vm, vm, vm],
        out_specs=vm,
        scratch_shapes=[
            pltpu.VMEM((16, 16, 128), F32),
            pltpu.VMEM((GROUP, 16, 128), F32),
            pltpu.VMEM((GROUP, 16, 128), F32),
            pltpu.VMEM((16, 16, 128), F32),
            pltpu.VMEM((16, 128), F32),
        ],
        name="scan_local",
    )(bc, dt, x, bias, a_log, reset_add)


def exchange_kernel(tile_ref, rate_ref, inc_ref, got, back, ret, s1, r1, s2, r2, l1, l2):
    seq = lax.axis_index("seq")
    tp = lax.axis_index("tp")
    barrier = pltpu.get_barrier_semaphore()

    def peer(off):
        return lax.rem(seq + off, SEQ)

    def hello(off, c):
        pl.semaphore_signal(barrier, inc=1, device_id=(peer(off), tp), device_id_type=MESH)
        return c

    lax.fori_loop(1, SEQ, hello, 0)
    pl.semaphore_wait(barrier, SEQ - 1)

    def out_copy(off):
        return pltpu.make_async_remote_copy(
            src_ref=tile_ref.at[peer(off)], dst_ref=got.at[seq], send_sem=s1.at[off], recv_sem=r1.at[off],
            device_id=(peer(off), tp), device_id_type=MESH,
        )

    def back_copy(off):
        return pltpu.make_async_remote_copy(
            src_ref=back.at[peer(off)], dst_ref=ret.at[seq], send_sem=s2.at[off], recv_sem=r2.at[off],
            device_id=(peer(off), tp), device_id_type=MESH,
        )

    def run(fn):
        def body(off, c):
            fn(off)
            return c

        lax.fori_loop(1, SEQ, body, 0)

    mine = pltpu.make_async_copy(tile_ref.at[seq], got.at[seq], l1)
    mine.start()
    run(lambda off: out_copy(off).start())
    mine.wait()
    run(lambda off: out_copy(off).wait_recv())

    rate = rate_ref[...]

    def chunk(i, state):
        back[i] = state
        tile = got[i]
        return jnp.exp2(tile[4:8] * rate) * state + tile[0:4]

    lax.fori_loop(0, SEQ, chunk, jnp.zeros((4, 128), F32), unroll=4)

    mine2 = pltpu.make_async_copy(back.at[seq], ret.at[seq], l2)
    mine2.start()
    run(lambda off: back_copy(off).start())
    mine2.wait()
    run(lambda off: back_copy(off).wait_recv())
    inc_ref[...] = ret[...]
    run(lambda off: out_copy(off).wait_send())
    run(lambda off: back_copy(off).wait_send())


def exchange(tiles, rate):
    vm = pl.BlockSpec(memory_space=pltpu.VMEM)
    dma = pltpu.SemaphoreType.DMA
    return pl.pallas_call(
        exchange_kernel,
        out_shape=jax.ShapeDtypeStruct((SEQ, 4, 128), F32),
        in_specs=[vm, vm],
        out_specs=vm,
        scratch_shapes=[
            pltpu.VMEM((SEQ, 8, 128), F32),
            pltpu.VMEM((SEQ, 4, 128), F32),
            pltpu.VMEM((SEQ, 4, 128), F32),
        ]
        + [dma((SEQ,)) for _ in range(4)]
        + [dma(()), dma(())],
        compiler_params=pltpu.CompilerParams(collective_id=1, has_side_effects=True),
        name="state_exchange",
    )(tiles, rate)


def final_kernel(bc_ref, dt_ref, x_ref, bias_ref, alog_ref, add_ref, skip_ref, inc_ref, out_ref, rate_s, step_s, u_s, state_s, y_s):
    rate_s[...] = (jnp.exp(alog_ref[...]) * (-LOG2E)).reshape(16, 16, 128)
    for n in range(16):
        for q in range(4):
            state_s[n, 4 * q : 4 * q + 4] = inc_ref[n * 4 + q]
    bias = bias_ref[...]
    skip = skip_ref[...]

    @pl.loop(0, TOK // GROUP)
    def _(g):
        x = fill_group(g, dt_ref, x_ref, bias, None, add_ref, step_s, u_s)

        def token(t, states):
            st = step_s[t]
            u = u_s[t]
            p = g * GROUP + t
            new = []
            acc = None
            for n in range(16):
                f = jnp.exp2(st * rate_s[n])
                s = f * states[n] + u * bc_ref[n, p]
                new.append(s)
                term = s * bc_ref[16 + n, p]
                acc = term if acc is None else acc + term
            y_s[t] = acc
            return tuple(new)

        states = lax.fori_loop(0, GROUP, token, tuple(state_s[n] for n in range(16)))
        for n in range(16):
            state_s[n] = states[n]
        rows = pl.ds(pl.multiple_of(g * GROUP, GROUP), GROUP)
        x = x_ref[rows, :].astype(F32)
        out_ref[rows, :] = (y_s[...].reshape(GROUP, 2048) + skip * x).astype(BF16)


def final_pass(bc, dt, x, bias, a_log, reset_add, skip, inc):
    vm = pl.BlockSpec(memory_space=pltpu.VMEM)
    sm = pl.BlockSpec(memory_space=pltpu.SMEM)
    return pl.pallas_call(
        final_kernel,
        out_shape=jax.ShapeDtypeStruct(x.shape, BF16),
        in_specs=[sm] + [vm] * 7,
        out_specs=vm,
        scratch_shapes=[
            pltpu.VMEM((16, 16, 128), F32),
            pltpu.VMEM((GROUP, 16, 128), F32),
            pltpu.VMEM((GROUP, 16, 128), F32),
            pltpu.VMEM((16, 16, 128), F32),
            pltpu.VMEM((GROUP, 16, 128), F32),
        ],
        name="scan_final",
    )(bc, dt, x, bias, a_log, reset_add, skip, inc)


ROWS = 256
PLANE = YN * TOK


def attend_kernel(meta_ref, q_ref, win_ref, res_ref, table_ref, ctx_ref, st_ref):
    z = meta_ref[0]
    base = meta_ref[1]
    first_start = meta_ref[2]
    planes = z - first_start // PLANE + 1
    scale = LOG2E / 128.0**0.5

    @pl.loop(0, 1024 // ROWS)
    def _(rt):
        rows = pl.ds(pl.multiple_of(rt * ROWS, ROWS), ROWS)
        q = q_ref[rows, :]
        pos = base + rt * (ROWS // 8) + lax.broadcasted_iota(jnp.int32, (ROWS, 1), 0) // 8
        start = jnp.zeros((ROWS, 1), jnp.int32)
        for r in range(4):
            start = jnp.where(pos >= meta_ref[4 + r], meta_ref[4 + r], start)

        def step(dz, carry):
            m, l, acc = carry
            k = win_ref[dz, :, 0].reshape(PLANE, 128)
            v = win_ref[dz, :, 1].reshape(PLANE, 128)
            s = lax.dot_general(q, k, (((1,), (1,)), ((), ())), preferred_element_type=F32)
            key_pos = (z - dz) * PLANE + lax.broadcasted_iota(jnp.int32, (1, PLANE), 1)
            ok = (key_pos <= pos) & (key_pos >= start)
            s = jnp.where(ok, s, NEG_FILL)
            m_new = jnp.maximum(m, jnp.max(s, axis=1, keepdims=True))
            e = jnp.exp2((s - m_new) * scale)
            fix = jnp.exp2((m - m_new) * scale)
            l = l * fix + jnp.sum(e, axis=1, keepdims=True)
            acc = acc * fix + jnp.dot(e.astype(BF16), v, preferred_element_type=F32)
            return m_new, l, acc

        init = (
            jnp.full((ROWS, 1), NEG_FILL, F32),
            jnp.zeros((ROWS, 1), F32),
            jnp.zeros((ROWS, 128), F32),
        )
        m, l, acc = lax.fori_loop(0, planes, step, init)
        ctx_ref[rows, :] = (acc / l).astype(BF16)

    tpos = base + lax.broadcasted_iota(jnp.int32, (TOK, 1), 0)
    add = jnp.zeros((TOK, 1024), F32)
    for r in range(4):
        vec = table_ref[pl.ds(meta_ref[8 + r], 1), :] * (meta_ref[12 + r].astype(F32) * 0.25)
        add = jnp.where(tpos >= meta_ref[4 + r], vec, add)
    st_ref[...] = (res_ref[...].astype(F32) + add).astype(BF16)


def attend(meta, q, win, residual, table):
    vm = pl.BlockSpec(memory_space=pltpu.VMEM)
    sm = pl.BlockSpec(memory_space=pltpu.SMEM)
    return pl.pallas_call(
        attend_kernel,
        out_shape=(jax.ShapeDtypeStruct(q.shape, BF16), jax.ShapeDtypeStruct(residual.shape, BF16)),
        in_specs=[sm, vm, vm, vm, vm],
        out_specs=(vm, vm),
        name="attend_steer",
    )(meta, q, win, residual, table)


def shards(residual, steer_table, steer_index, steer_num, lengths, queries, keys, values, inner_x, dt_raw, dt_bias, a_log, skip_gain, bc_weight):
    seq = lax.axis_index("seq")
    base = seq * TOK
    ends = jnp.cumsum(lengths).astype(jnp.int32)
    starts = ends - lengths
    positions = base + jnp.arange(TOK, dtype=jnp.int32)
    is_reset = jnp.any(positions[:, None] == starts[None, :], axis=1)
    reset_add = jnp.where(is_reset, RESET, 0.0).astype(F32)[:, None]
    first_start = jnp.max(jnp.where(starts <= base, starts, 0))
    meta = jnp.concatenate(
        [jnp.stack([seq // YN, base, first_start, 0]).astype(jnp.int32), starts, steer_index, steer_num]
    )
    kv = jnp.stack([keys[:, 0], values[:, 0]])
    win, bc = gather(kv, inner_x, bc_weight)
    bias = dt_bias[None, :]
    tiles = local_pass(bc, dt_raw, inner_x, bias, a_log, reset_add)
    rate = lax.dynamic_slice(a_log, (seq // 4, lax.rem(seq, 4) * 512), (1, 512)).reshape(4, 128)
    inc = exchange(tiles, jnp.exp(rate) * (-LOG2E))
    mixed = final_pass(bc, dt_raw, inner_x, bias, a_log, reset_add, skip_gain[None, :], inc)
    ctx, steered = attend(meta, queries.reshape(1024, 128), win, residual, steer_table.astype(F32))
    return steered, ctx.reshape(queries.shape), mixed


def solution(mesh):
    return jax.shard_map(
        shards,
        mesh=mesh,
        in_specs=(
            P("seq", "tp"),
            P(None, "tp"),
            P(),
            P(),
            P(),
            P("seq", "tp", None),
            P("seq", "tp", None),
            P("seq", "tp", None),
            P("seq", "tp"),
            P("seq", "tp"),
            P("tp"),
            P(None, "tp"),
            P("tp"),
            P(None, "tp"),
        ),
        out_specs=(P("seq", "tp"), P("seq", "tp", None), P("seq", "tp")),
        check_vma=False,
    )
```

```python
import functools
import jax
import jax.numpy as jnp
from jax import lax
from jax.experimental import pallas as pl
from jax.experimental.pallas import tpu as pltpu
from jax.sharding import PartitionSpec as P

LOG2E = 1.4426950408889634
NEG_FILL = -1e30
RESET = 1e30
YN = 4
ZN = 16
SEQ = YN * ZN
TPN = 8
WIN = 8
TOK = 128
GROUP = 16
MESH = pl.DeviceIdType.MESH
F32 = jnp.float32
BF16 = jnp.bfloat16


def starts_of(len_ref):
    s1 = len_ref[0]
    s2 = s1 + len_ref[1]
    s3 = s2 + len_ref[2]
    return (jnp.int32(0), s1, s2, s3)


def log1p_exp(v):
    return jnp.maximum(v, 0.0) + jnp.log1p(jnp.exp(-jnp.abs(v)))


def fill_group(g, base, starts, dt_ref, x_ref, bias, step_s, u_s):
    rows = pl.ds(pl.multiple_of(g * GROUP, GROUP), GROUP)
    raw = dt_ref[rows, :].astype(F32)
    x = x_ref[rows, :].astype(F32)
    step = log1p_exp(raw + bias)
    pos = base + g * GROUP + lax.broadcasted_iota(jnp.int32, (GROUP, 1), 0)
    hit = (pos == starts[0]) | (pos == starts[1]) | (pos == starts[2]) | (pos == starts[3])
    u_s[...] = (step * x).reshape(GROUP, 16, 128)
    step_s[...] = (step + jnp.where(hit, RESET, 0.0)).reshape(GROUP, 16, 128)


def main_kernel(
    len_ref, k_ref, v_ref, x_ref, w_ref, dt_ref, bias_ref, alog_ref,
    win_ref, bc_ref, inc_ref,
    parts, bc_s, rate_s, step_s, u_s, msg, ych, zout, zin, outb, inc_s,
    own_sem, bc_sem, zs, zr, rs, rr, ls, lr, ks, kr, vs, vr, bs, br, ps, pr, qs, qr, fs, fr,
):
    seq = lax.axis_index("seq")
    tp = lax.axis_index("tp")
    z = seq // YN
    y = lax.rem(seq, YN)
    left_y = lax.rem(y + YN - 1, YN)
    right_y = lax.rem(y + 1, YN)

    def zy(dz, dy):
        return lax.rem(z + dz, ZN) * YN + lax.rem(y + dy, YN)

    up = zy(1, 0)
    right = zy(0, 1)
    left = zy(0, YN - 1)

    barrier = pltpu.get_barrier_semaphore()
    for dz in (1, 2, 4, ZN - 1, ZN - 2, ZN - 4):
        pl.semaphore_signal(barrier, inc=1, device_id=(zy(dz, 0), tp), device_id_type=MESH)
    for dy in range(1, YN):
        pl.semaphore_signal(barrier, inc=1, device_id=(zy(0, dy), tp), device_id_type=MESH)
    for off in range(1, TPN):
        pl.semaphore_signal(barrier, inc=1, device_id=(seq, lax.rem(tp + off, TPN)), device_id_type=MESH)
    pl.semaphore_wait(barrier, 6 + YN - 1 + TPN - 1)

    def remote(src, dst, ssem, rsem, peer):
        return pltpu.make_async_remote_copy(
            src_ref=src, dst_ref=dst, send_sem=ssem, recv_sem=rsem, device_id=(peer, tp), device_id_type=MESH
        )

    def block(s, h):
        return (k_ref, v_ref)[h] if s == 0 else win_ref.at[s, y, h]

    def z_copy(s, h):
        return remote(block(s - 1, h), win_ref.at[s, y, h], zs.at[h, s], zr.at[h, s], up)

    def right_copy(s, h):
        return remote(block(s, h), win_ref.at[s, y, h], rs.at[h, s], rr.at[h, s], right)

    def left_copy(s, h):
        return remote(block(s, h), win_ref.at[s, y, h], ls.at[h, s], lr.at[h, s], left)

    def k_copy(s):
        return remote(win_ref.at[s, left_y, 0], win_ref.at[s, left_y, 0], ks.at[s], kr.at[s], right)

    def v_copy(s):
        return remote(win_ref.at[s, right_y, 1], win_ref.at[s, right_y, 1], vs.at[s], vr.at[s], left)

    def spread(s):
        right_copy(s - 1, 0).wait_recv()
        k_copy(s - 1).start()
        left_copy(s - 1, 1).wait_recv()
        v_copy(s - 1).start()

    def kv_step(s):
        for h in (0, 1):
            z_copy(s, h).wait_recv()
            if s < WIN:
                z_copy(s + 1, h).start()
            right_copy(s, h).start()
            left_copy(s, h).start()
        spread(s)

    own = [pltpu.make_async_copy((k_ref, v_ref)[h], win_ref.at[0, y, h], own_sem.at[h]) for h in (0, 1)]
    for h in (0, 1):
        z_copy(1, h).start()
    for h in (0, 1):
        right_copy(0, h).start()
        left_copy(0, h).start()
        own[h].start()

    parts[tp] = lax.dot_general(w_ref[...], x_ref[...], (((1,), (1,)), ((), ())), preferred_element_type=F32)

    def bc_copy(off):
        return pltpu.make_async_remote_copy(
            src_ref=parts.at[tp], dst_ref=parts.at[tp], send_sem=bs.at[off], recv_sem=br.at[off],
            device_id=(seq, lax.rem(tp + off, TPN)), device_id_type=MESH,
        )

    for off in range(1, TPN):
        bc_copy(off).start()

    rate_s[...] = (jnp.exp(alog_ref[...]) * (-LOG2E)).reshape(16, 16, 128)
    msg[...] = jnp.zeros_like(msg)
    bias = bias_ref[...]
    base = seq * TOK
    starts = starts_of(len_ref)
    kv_step(1)
    for off in range(1, TPN):
        bc_copy(off).wait_recv()
    total_bc = parts[0]
    for t in range(1, TPN):
        total_bc = total_bc + parts[t]
    bc_ref[...] = total_bc
    to_smem = pltpu.make_async_copy(bc_ref, bc_s, bc_sem)
    to_smem.start()
    to_smem.wait()

    def scan_groups(lo, hi):
        @pl.loop(lo, hi)
        def _(g):
            fill_group(g, base, starts, dt_ref, x_ref, bias, step_s, u_s)

            def token(t, carry):
                states, total = carry
                st = step_s[t]
                u = u_s[t]
                p = g * GROUP + t
                new = []
                for n in range(16):
                    f = jnp.exp2(st * rate_s[n])
                    new.append(f * states[n] + u * bc_s[n, p])
                return tuple(new), total + st

            init = (tuple(msg[n // 4, n % 4] for n in range(16)), msg[0, 4])
            states, total = lax.fori_loop(0, GROUP, token, init, unroll=2)
            for n in range(16):
                msg[n // 4, n % 4] = states[n]
            msg[0, 4] = total

    scan_groups(0, 3)
    kv_step(2)
    scan_groups(3, 6)
    kv_step(3)
    scan_groups(6, 8)
    total = msg[0, 4]
    for q in range(1, 4):
        msg[q, 4] = total

    def part_copy(d):
        return remote(msg.at[lax.rem(y + d, YN)], ych.at[y], ps.at[d], pr.at[d], zy(0, d))

    for d in (1, 3, 2):
        part_copy(d).start()
    ych[y] = msg[y]
    kv_step(4)
    for d in range(1, YN):
        part_copy(d).wait_recv()
    rate = rate_s[pl.ds(4 * y, 4)]
    acc = ych[0, 0:4]
    dec = ych[0, 4]
    for c in range(1, YN):
        acc = jnp.exp2(rate * ych[c, 4][None]) * acc + ych[c, 0:4]
        dec = dec + ych[c, 4]

    def z_round(j, d):
        return remote(zout.at[j], zin.at[j], qs.at[j], qr.at[j], zy(d, 0))

    for j, d in enumerate((1, 1, 2, 4)):
        zout[j, 0:4] = acc
        zout[j, 4] = dec
        z_round(j, d).start()
        kv_step(5 + j)
        z_round(j, d).wait_recv()
        here = (z >= d).astype(F32)
        got = zin[j, 0:4] * here
        got_dec = zin[j, 4] * here
        if j == 0:
            acc, dec = got, got_dec
        else:
            acc = acc + jnp.exp2(rate * dec[None]) * got
            dec = dec + got_dec

    for c in range(YN):
        outb[c] = acc
        if c < YN - 1:
            acc = jnp.exp2(rate * ych[c, 4][None]) * acc + ych[c, 0:4]

    def back_copy(d):
        return remote(outb.at[lax.rem(y + d, YN)], inc_s.at[y], fs.at[d], fr.at[d], zy(0, d))

    for d in (1, 3, 2):
        back_copy(d).start()
    inc_s[y] = outb[y]
    spread(WIN + 1)
    for d in range(1, YN):
        back_copy(d).wait_recv()
    inc_ref[...] = inc_s[...]

    for h in (0, 1):
        own[h].wait()
    for off in range(1, TPN):
        bc_copy(off).wait_send()
    for d in range(1, YN):
        part_copy(d).wait_send()
        back_copy(d).wait_send()
    for j, d in enumerate((1, 1, 2, 4)):
        z_round(j, d).wait_send()
    for s in range(WIN + 1):
        for h in (0, 1):
            if s > 0:
                z_copy(s, h).wait_send()
            right_copy(s, h).wait_send()
            left_copy(s, h).wait_send()
        right_copy(s, 1).wait_recv()
        left_copy(s, 0).wait_recv()
        k_copy(s).wait()
        v_copy(s).wait()


def main_pass(lengths, k, v, x, w, dt, bias, a_log):
    vm = pl.BlockSpec(memory_space=pltpu.VMEM)
    sm = pl.BlockSpec(memory_space=pltpu.SMEM)
    dma = pltpu.SemaphoreType.DMA
    n = WIN + 1
    return pl.pallas_call(
        main_kernel,
        out_shape=(
            jax.ShapeDtypeStruct((n, YN, 2, TOK, 128), BF16),
            jax.ShapeDtypeStruct((32, TOK), F32),
            jax.ShapeDtypeStruct((YN, 4, 16, 128), F32),
        ),
        in_specs=[sm] + [vm] * 7,
        out_specs=(pl.BlockSpec(memory_space=pl.ANY), vm, vm),
        scratch_shapes=[
            pltpu.VMEM((TPN, 32, TOK), F32),
            pltpu.SMEM((32, TOK), F32),
            pltpu.VMEM((16, 16, 128), F32),
            pltpu.VMEM((GROUP, 16, 128), F32),
            pltpu.VMEM((GROUP, 16, 128), F32),
            pltpu.VMEM((YN, 5, 16, 128), F32),
            pltpu.VMEM((YN, 5, 16, 128), F32),
            pltpu.VMEM((4, 5, 16, 128), F32),
            pltpu.VMEM((4, 5, 16, 128), F32),
            pltpu.VMEM((YN, 4, 16, 128), F32),
            pltpu.VMEM((YN, 4, 16, 128), F32),
            dma((2,)),
            dma(()),
        ]
        + [dma((2, n)) for _ in range(6)]
        + [dma((n,)) for _ in range(4)]
        + [dma((TPN,)), dma((TPN,))]
        + [dma((4,)) for _ in range(6)],
        compiler_params=pltpu.CompilerParams(collective_id=0, has_side_effects=True),
        name="gather_scan_exchange",
    )(lengths, k, v, x, w, dt, bias, a_log)


def final_kernel(len_ref, bc_ref, dt_ref, x_ref, bias_ref, alog_ref, skip_ref, inc_ref, out_ref, rate_s, step_s, u_s, state_s, y_s):
    base = lax.axis_index("seq") * TOK
    starts = starts_of(len_ref)
    rate_s[...] = (jnp.exp(alog_ref[...]) * (-LOG2E)).reshape(16, 16, 128)
    for n in range(16):
        state_s[n] = inc_ref[n // 4, n % 4]
    bias = bias_ref[...]
    skip = skip_ref[...]

    @pl.loop(0, TOK // GROUP)
    def _(g):
        fill_group(g, base, starts, dt_ref, x_ref, bias, step_s, u_s)

        def token(t, states):
            st = step_s[t]
            u = u_s[t]
            p = g * GROUP + t
            new = []
            acc = None
            for n in range(16):
                f = jnp.exp2(st * rate_s[n])
                s = f * states[n] + u * bc_ref[n, p]
                new.append(s)
                term = s * bc_ref[16 + n, p]
                acc = term if acc is None else acc + term
            y_s[t] = acc
            return tuple(new)

        states = lax.fori_loop(0, GROUP, token, tuple(state_s[n] for n in range(16)), unroll=2)
        for n in range(16):
            state_s[n] = states[n]
        rows = pl.ds(pl.multiple_of(g * GROUP, GROUP), GROUP)
        x = x_ref[rows, :].astype(F32)
        out_ref[rows, :] = (y_s[...].reshape(GROUP, 2048) + skip * x).astype(BF16)


def final_pass(lengths, bc, dt, x, bias, a_log, skip, inc):
    vm = pl.BlockSpec(memory_space=pltpu.VMEM)
    sm = pl.BlockSpec(memory_space=pltpu.SMEM)
    return pl.pallas_call(
        final_kernel,
        out_shape=jax.ShapeDtypeStruct(x.shape, BF16),
        in_specs=[sm, sm] + [vm] * 6,
        out_specs=vm,
        scratch_shapes=[
            pltpu.VMEM((16, 16, 128), F32),
            pltpu.VMEM((GROUP, 16, 128), F32),
            pltpu.VMEM((GROUP, 16, 128), F32),
            pltpu.VMEM((16, 16, 128), F32),
            pltpu.VMEM((GROUP, 16, 128), F32),
        ],
        name="scan_final",
    )(lengths, bc, dt, x, bias, a_log, skip, inc)


ROWS = 256
PLANE = YN * TOK


def attend_kernel(len_ref, idx_ref, num_ref, q_ref, win_ref, res_ref, table_ref, ctx_ref, st_ref):
    seq = lax.axis_index("seq")
    z = seq // YN
    base = seq * TOK
    starts = starts_of(len_ref)
    first_start = jnp.int32(0)
    for r in range(1, 4):
        first_start = jnp.where(starts[r] <= base, starts[r], first_start)
    planes = z - first_start // PLANE + 1
    scale = LOG2E / 128.0**0.5

    @pl.loop(0, 1024 // ROWS)
    def _(rt):
        rows = pl.ds(pl.multiple_of(rt * ROWS, ROWS), ROWS)
        q = q_ref[rows, :]
        pos = base + rt * (ROWS // 8) + lax.broadcasted_iota(jnp.int32, (ROWS, 1), 0) // 8
        start = jnp.zeros((ROWS, 1), jnp.int32)
        for r in range(4):
            start = jnp.where(pos >= starts[r], starts[r], start)

        def step(dz, carry):
            m, l, acc = carry
            k = win_ref[dz, :, 0].reshape(PLANE, 128)
            v = win_ref[dz, :, 1].reshape(PLANE, 128)
            s = lax.dot_general(q, k, (((1,), (1,)), ((), ())), preferred_element_type=F32)
            key_pos = (z - dz) * PLANE + lax.broadcasted_iota(jnp.int32, (1, PLANE), 1)
            ok = (key_pos <= pos) & (key_pos >= start)
            s = jnp.where(ok, s, NEG_FILL)
            m_new = jnp.maximum(m, jnp.max(s, axis=1, keepdims=True))
            e = jnp.exp2((s - m_new) * scale)
            fix = jnp.exp2((m - m_new) * scale)
            l = l * fix + jnp.sum(e, axis=1, keepdims=True)
            acc = acc * fix + jnp.dot(e.astype(BF16), v, preferred_element_type=F32)
            return m_new, l, acc

        init = (
            jnp.full((ROWS, 1), NEG_FILL, F32),
            jnp.zeros((ROWS, 1), F32),
            jnp.zeros((ROWS, 128), F32),
        )
        m, l, acc = lax.fori_loop(0, planes, step, init)
        ctx_ref[rows, :] = (acc / l).astype(BF16)

    tpos = base + lax.broadcasted_iota(jnp.int32, (TOK, 1), 0)
    add = jnp.zeros((TOK, 1024), F32)
    table = table_ref[...].astype(F32)
    for r in range(4):
        vec = jnp.zeros((1, 1024), F32)
        for i in range(7):
            vec = jnp.where(idx_ref[r] == i, table[i : i + 1], vec)
        add = jnp.where(tpos >= starts[r], vec * (num_ref[r].astype(F32) * 0.25), add)
    st_ref[...] = (res_ref[...].astype(F32) + add).astype(BF16)


def attend(lengths, index, num, q, win, residual, table):
    vm = pl.BlockSpec(memory_space=pltpu.VMEM)
    sm = pl.BlockSpec(memory_space=pltpu.SMEM)
    return pl.pallas_call(
        attend_kernel,
        out_shape=(jax.ShapeDtypeStruct(q.shape, BF16), jax.ShapeDtypeStruct(residual.shape, BF16)),
        in_specs=[sm, sm, sm, vm, vm, vm, vm],
        out_specs=(vm, vm),
        name="attend_steer",
    )(lengths, index, num, q, win, residual, table)


def shards(residual, steer_table, steer_index, steer_num, lengths, queries, keys, values, inner_x, dt_raw, dt_bias, a_log, skip_gain, bc_weight):
    bias = dt_bias[None, :]
    k = keys.reshape(TOK, 128)
    v = values.reshape(TOK, 128)
    win, bc, inc = main_pass(lengths, k, v, inner_x, bc_weight, dt_raw, bias, a_log)
    ctx, steered = attend(lengths, steer_index, steer_num, queries.reshape(1024, 128), win, residual, steer_table)
    mixed = final_pass(lengths, bc, dt_raw, inner_x, bias, a_log, skip_gain[None, :], inc)
    return steered, ctx.reshape(queries.shape), mixed


def solution(mesh):
    return jax.shard_map(
        shards,
        mesh=mesh,
        in_specs=(
            P("seq", "tp"),
            P(None, "tp"),
            P(),
            P(),
            P(),
            P("seq", "tp", None),
            P("seq", "tp", None),
            P("seq", "tp", None),
            P("seq", "tp"),
            P("seq", "tp"),
            P("tp"),
            P(None, "tp"),
            P("tp"),
            P(None, "tp"),
        ),
        out_specs=(P("seq", "tp"), P("seq", "tp", None), P("seq", "tp")),
        check_vma=False,
    )
```

```python
import functools
import jax
import jax.numpy as jnp
from jax import lax
from jax.experimental import pallas as pl
from jax.experimental.pallas import tpu as pltpu
from jax.sharding import PartitionSpec as P

LOG2E = 1.4426950408889634
NEG_FILL = -1e30
RESET = 1e30
YN = 4
ZN = 16
SEQ = YN * ZN
TPN = 8
WIN = 8
TOK = 128
ROWS = 256
PLANE = YN * TOK
GROUP = 16
MESH = pl.DeviceIdType.MESH
F32 = jnp.float32
BF16 = jnp.bfloat16


def starts_of(len_ref):
    s1 = len_ref[0]
    s2 = s1 + len_ref[1]
    s3 = s2 + len_ref[2]
    return (jnp.int32(0), s1, s2, s3)


def log1p_exp(v):
    return jnp.maximum(v, 0.0) + jnp.log1p(jnp.exp(-jnp.abs(v)))


def fill_group(g, base, starts, dt_ref, x_ref, bias, step_s, u_s):
    rows = pl.ds(pl.multiple_of(g * GROUP, GROUP), GROUP)
    raw = dt_ref[rows, :].astype(F32)
    x = x_ref[rows, :].astype(F32)
    step = log1p_exp(raw + bias)
    pos = base + g * GROUP + lax.broadcasted_iota(jnp.int32, (GROUP, 1), 0)
    hit = (pos == starts[0]) | (pos == starts[1]) | (pos == starts[2]) | (pos == starts[3])
    u_s[pl.ds(g * GROUP, GROUP)] = (step * x).reshape(GROUP, 16, 128)
    step_s[...] = (step + jnp.where(hit, RESET, 0.0)).reshape(GROUP, 16, 128)


def main_kernel(
    len_ref, idx_ref, num_ref, k_ref, v_ref, x_ref, w_ref, dt_ref, bias_ref, alog_ref, skip_ref, q_ref, res_ref, table_ref,
    ctx_ref, st_ref, out_ref,
    win_ref, parts, bc_v, bc_s, rate_s, step_s, u_s, fac_s, msg, ych, zout, zin, outb, inc_s, y_s, start_s, m_s, l_s, acc_s,
    own_sem, bc_sem, zs, zr, rs, rr, ls, lr, ks, kr, vs, vr, bs, br, ps, pr, qs, qr, fs, fr,
):
    seq = lax.axis_index("seq")
    tp = lax.axis_index("tp")
    z = seq // YN
    y = lax.rem(seq, YN)
    left_y = lax.rem(y + YN - 1, YN)
    right_y = lax.rem(y + 1, YN)

    def zy(dz, dy):
        return lax.rem(z + dz, ZN) * YN + lax.rem(y + dy, YN)

    up = zy(1, 0)
    right = zy(0, 1)
    left = zy(0, YN - 1)

    barrier = pltpu.get_barrier_semaphore()
    for dz in (1, 2, 4, ZN - 1, ZN - 2, ZN - 4):
        pl.semaphore_signal(barrier, inc=1, device_id=(zy(dz, 0), tp), device_id_type=MESH)
    for dy in range(1, YN):
        pl.semaphore_signal(barrier, inc=1, device_id=(zy(0, dy), tp), device_id_type=MESH)
    for off in range(1, TPN):
        pl.semaphore_signal(barrier, inc=1, device_id=(seq, lax.rem(tp + off, TPN)), device_id_type=MESH)
    pl.semaphore_wait(barrier, 6 + YN - 1 + TPN - 1)

    def remote(src, dst, ssem, rsem, peer):
        return pltpu.make_async_remote_copy(
            src_ref=src, dst_ref=dst, send_sem=ssem, recv_sem=rsem, device_id=(peer, tp), device_id_type=MESH
        )

    def block(s, h):
        return (k_ref, v_ref)[h] if s == 0 else win_ref.at[s, y, h]

    def z_copy(s, h):
        return remote(block(s - 1, h), win_ref.at[s, y, h], zs.at[h, s], zr.at[h, s], up)

    def right_copy(s, h):
        return remote(block(s, h), win_ref.at[s, y, h], rs.at[h, s], rr.at[h, s], right)

    def left_copy(s, h):
        return remote(block(s, h), win_ref.at[s, y, h], ls.at[h, s], lr.at[h, s], left)

    def k_copy(s):
        return remote(win_ref.at[s, left_y, 0], win_ref.at[s, left_y, 0], ks.at[s], kr.at[s], right)

    def v_copy(s):
        return remote(win_ref.at[s, right_y, 1], win_ref.at[s, right_y, 1], vs.at[s], vr.at[s], left)

    def spread(s):
        right_copy(s - 1, 0).wait_recv()
        k_copy(s - 1).start()
        left_copy(s - 1, 1).wait_recv()
        v_copy(s - 1).start()

    def kv_step(s):
        for h in (0, 1):
            z_copy(s, h).wait_recv()
            if s < WIN:
                z_copy(s + 1, h).start()
            right_copy(s, h).start()
            left_copy(s, h).start()
        spread(s)

    own = [pltpu.make_async_copy((k_ref, v_ref)[h], win_ref.at[0, y, h], own_sem.at[h]) for h in (0, 1)]
    for h in (0, 1):
        z_copy(1, h).start()
    for h in (0, 1):
        right_copy(0, h).start()
        left_copy(0, h).start()
        own[h].start()

    parts[tp] = lax.dot_general(w_ref[...], x_ref[...], (((1,), (1,)), ((), ())), preferred_element_type=F32)

    def bc_copy(off):
        return pltpu.make_async_remote_copy(
            src_ref=parts.at[tp], dst_ref=parts.at[tp], send_sem=bs.at[off], recv_sem=br.at[off],
            device_id=(seq, lax.rem(tp + off, TPN)), device_id_type=MESH,
        )

    for off in range(1, TPN):
        bc_copy(off).start()

    rate_s[...] = (jnp.exp(alog_ref[...]) * (-LOG2E)).reshape(16, 16, 128)
    msg[...] = jnp.zeros_like(msg)
    bias = bias_ref[...]
    base = seq * TOK
    starts = starts_of(len_ref)
    scale = LOG2E / 128.0**0.5

    def ready(dz):
        right_copy(dz, 1).wait_recv()
        left_copy(dz, 0).wait_recv()
        k_copy(dz).wait_recv()
        v_copy(dz).wait_recv()

    def attend_plane(dz):
        ready(dz)

        @pl.when(z >= dz)
        def _():
            @pl.loop(0, 1024 // ROWS)
            def _(rt):
                rows = pl.ds(pl.multiple_of(rt * ROWS, ROWS), ROWS)
                key_pos = lax.broadcasted_iota(jnp.int32, (1, PLANE), 1)
                first = start_s[rows, :] - (z - dz) * PLANE
                kk = win_ref[dz, :, 0].reshape(PLANE, 128)
                vv = win_ref[dz, :, 1].reshape(PLANE, 128)
                sc = lax.dot_general(q_ref[rows, :], kk, (((1,), (1,)), ((), ())), preferred_element_type=F32)
                ok = key_pos >= first
                if dz == 0:
                    last = y * TOK + rt * (ROWS // 8) + lax.broadcasted_iota(jnp.int32, (ROWS, 1), 0) // 8
                    ok = ok & (key_pos <= last)
                sc = jnp.where(ok, sc, NEG_FILL)
                top = jnp.max(sc, axis=1, keepdims=True)
                if dz == 0:
                    e = jnp.exp2((sc - top) * scale)
                    l_s[rows, :] = jnp.sum(e, axis=1, keepdims=True)
                    acc_s[rows, :] = jnp.dot(e.astype(BF16), vv, preferred_element_type=F32)
                    m_s[rows, :] = top
                else:
                    old = m_s[rows, :]
                    top = jnp.maximum(old, top)
                    e = jnp.exp2((sc - top) * scale)
                    fix = jnp.exp2((old - top) * scale)
                    l_s[rows, :] = l_s[rows, :] * fix + jnp.sum(e, axis=1, keepdims=True)
                    acc_s[rows, :] = acc_s[rows, :] * fix + jnp.dot(e.astype(BF16), vv, preferred_element_type=F32)
                    m_s[rows, :] = top

    qpos = base + lax.broadcasted_iota(jnp.int32, (1024, 1), 0) // 8
    qstart = jnp.zeros((1024, 1), jnp.int32)
    for r in range(1, 4):
        qstart = jnp.where(qpos >= starts[r], starts[r], qstart)
    start_s[...] = qstart

    table = table_ref[...].astype(F32)
    tpos = base + lax.broadcasted_iota(jnp.int32, (TOK, 1), 0)
    add = jnp.zeros((TOK, 1024), F32)
    for r in range(4):
        vec = jnp.zeros((1, 1024), F32)
        for i in range(7):
            vec = jnp.where(idx_ref[r] == i, table[i : i + 1], vec)
        add = jnp.where(tpos >= starts[r], vec * (num_ref[r].astype(F32) * 0.25), add)
    st_ref[...] = (res_ref[...].astype(F32) + add).astype(BF16)

    kv_step(1)
    for off in range(1, TPN):
        bc_copy(off).wait_recv()
    total_bc = parts[0]
    for t in range(1, TPN):
        total_bc = total_bc + parts[t]
    bc_v[...] = total_bc
    to_smem = pltpu.make_async_copy(bc_v, bc_s, bc_sem)
    to_smem.start()
    to_smem.wait()

    def scan_groups(lo, hi):
        @pl.loop(lo, hi)
        def _(g):
            fill_group(g, base, starts, dt_ref, x_ref, bias, step_s, u_s)

            def token(t, carry):
                states, total = carry
                st = step_s[t]
                p = g * GROUP + t
                u = u_s[p]
                new = []
                for n in range(16):
                    f = jnp.exp2(st * rate_s[n])
                    fac_s[p, n] = f
                    new.append(f * states[n] + u * bc_s[n, p])
                return tuple(new), total + st

            init = (tuple(msg[n // 4, n % 4] for n in range(16)), msg[0, 4])
            states, total = lax.fori_loop(0, GROUP, token, init, unroll=2)
            for n in range(16):
                msg[n // 4, n % 4] = states[n]
            msg[0, 4] = total

    scan_groups(0, 3)
    kv_step(2)
    scan_groups(3, 6)
    kv_step(3)
    scan_groups(6, 8)
    total = msg[0, 4]
    for q in range(1, 4):
        msg[q, 4] = total

    def part_copy(d):
        return remote(msg.at[lax.rem(y + d, YN)], ych.at[y], ps.at[d], pr.at[d], zy(0, d))

    for d in (1, 3, 2):
        part_copy(d).start()
    ych[y] = msg[y]
    kv_step(4)
    for h in (0, 1):
        own[h].wait()
    attend_plane(0)
    attend_plane(1)
    for d in range(1, YN):
        part_copy(d).wait_recv()
    rate = rate_s[pl.ds(4 * y, 4)]
    acc = ych[0, 0:4]
    dec = ych[0, 4]
    for c in range(1, YN):
        acc = jnp.exp2(rate * ych[c, 4][None]) * acc + ych[c, 0:4]
        dec = dec + ych[c, 4]

    def z_round(j, d):
        return remote(zout.at[j], zin.at[j], qs.at[j], qr.at[j], zy(d, 0))

    for j, d in enumerate((1, 1, 2, 4)):
        zout[j, 0:4] = acc
        zout[j, 4] = dec
        z_round(j, d).start()
        kv_step(5 + j)
        for dz in ((), (2,), (3, 4), (5, 6))[j]:
            attend_plane(dz)
        z_round(j, d).wait_recv()
        here = (z >= d).astype(F32)
        got = zin[j, 0:4] * here
        got_dec = zin[j, 4] * here
        if j == 0:
            acc, dec = got, got_dec
        else:
            acc = acc + jnp.exp2(rate * dec[None]) * got
            dec = dec + got_dec

    for c in range(YN):
        outb[c] = acc
        if c < YN - 1:
            acc = jnp.exp2(rate * ych[c, 4][None]) * acc + ych[c, 0:4]

    def back_copy(d):
        return remote(outb.at[lax.rem(y + d, YN)], inc_s.at[y], fs.at[d], fr.at[d], zy(0, d))

    for d in (1, 3, 2):
        back_copy(d).start()
    inc_s[y] = outb[y]
    spread(WIN + 1)
    attend_plane(7)
    attend_plane(8)
    ctx_ref[...] = (acc_s[...] / l_s[...]).astype(BF16)
    for d in range(1, YN):
        back_copy(d).wait_recv()
    skip = skip_ref[...]

    @pl.loop(0, TOK // GROUP)
    def _(g):
        def token(t, states):
            p = g * GROUP + t
            u = u_s[p]
            new = []
            total = None
            for n in range(16):
                state = fac_s[p, n] * states[n] + u * bc_s[n, p]
                new.append(state)
                term = state * bc_s[16 + n, p]
                total = term if total is None else total + term
            y_s[t] = total
            return tuple(new)

        states = lax.fori_loop(0, GROUP, token, tuple(inc_s[n // 4, n % 4] for n in range(16)), unroll=2)
        for n in range(16):
            inc_s[n // 4, n % 4] = states[n]
        rows = pl.ds(pl.multiple_of(g * GROUP, GROUP), GROUP)
        x = x_ref[rows, :].astype(F32)
        out_ref[rows, :] = (y_s[...].reshape(GROUP, 2048) + skip * x).astype(BF16)

    for off in range(1, TPN):
        bc_copy(off).wait_send()
    for d in range(1, YN):
        part_copy(d).wait_send()
        back_copy(d).wait_send()
    for j, d in enumerate((1, 1, 2, 4)):
        z_round(j, d).wait_send()
    for s in range(WIN + 1):
        for h in (0, 1):
            if s > 0:
                z_copy(s, h).wait_send()
            right_copy(s, h).wait_send()
            left_copy(s, h).wait_send()
        k_copy(s).wait_send()
        v_copy(s).wait_send()


def main_pass(*args):
    vm = pl.BlockSpec(memory_space=pltpu.VMEM)
    sm = pl.BlockSpec(memory_space=pltpu.SMEM)
    dma = pltpu.SemaphoreType.DMA
    n = WIN + 1
    return pl.pallas_call(
        main_kernel,
        out_shape=(
            jax.ShapeDtypeStruct((1024, 128), BF16),
            jax.ShapeDtypeStruct((TOK, 1024), BF16),
            jax.ShapeDtypeStruct((TOK, 2048), BF16),
        ),
        in_specs=[sm] * 3 + [vm] * 11,
        out_specs=(vm, vm, vm),
        scratch_shapes=[
            pltpu.VMEM((n, YN, 2, TOK, 128), BF16),
            pltpu.VMEM((TPN, 32, TOK), F32),
            pltpu.VMEM((32, TOK), F32),
            pltpu.SMEM((32, TOK), F32),
            pltpu.VMEM((16, 16, 128), F32),
            pltpu.VMEM((GROUP, 16, 128), F32),
            pltpu.VMEM((TOK, 16, 128), F32),
            pltpu.VMEM((TOK, 16, 16, 128), F32),
            pltpu.VMEM((YN, 5, 16, 128), F32),
            pltpu.VMEM((YN, 5, 16, 128), F32),
            pltpu.VMEM((4, 5, 16, 128), F32),
            pltpu.VMEM((4, 5, 16, 128), F32),
            pltpu.VMEM((YN, 4, 16, 128), F32),
            pltpu.VMEM((YN, 4, 16, 128), F32),
            pltpu.VMEM((GROUP, 16, 128), F32),
            pltpu.VMEM((1024, 1), jnp.int32),
            pltpu.VMEM((1024, 1), F32),
            pltpu.VMEM((1024, 1), F32),
            pltpu.VMEM((1024, 128), F32),
            dma((2,)),
            dma(()),
        ]
        + [dma((2, n)) for _ in range(6)]
        + [dma((n,)) for _ in range(4)]
        + [dma((TPN,)), dma((TPN,))]
        + [dma((4,)) for _ in range(6)],
        compiler_params=pltpu.CompilerParams(collective_id=0, has_side_effects=True),
        name="layer",
    )(*args)


def shards(residual, steer_table, steer_index, steer_num, lengths, queries, keys, values, inner_x, dt_raw, dt_bias, a_log, skip_gain, bc_weight):
    ctx, steered, mixed = main_pass(
        lengths,
        steer_index,
        steer_num,
        keys.reshape(TOK, 128),
        values.reshape(TOK, 128),
        inner_x,
        bc_weight,
        dt_raw,
        dt_bias[None, :],
        a_log,
        skip_gain[None, :],
        queries.reshape(1024, 128),
        residual,
        steer_table,
    )
    return steered, ctx.reshape(queries.shape), mixed


def solution(mesh):
    return jax.shard_map(
        shards,
        mesh=mesh,
        in_specs=(
            P("seq", "tp"),
            P(None, "tp"),
            P(),
            P(),
            P(),
            P("seq", "tp", None),
            P("seq", "tp", None),
            P("seq", "tp", None),
            P("seq", "tp"),
            P("seq", "tp"),
            P("tp"),
            P(None, "tp"),
            P("tp"),
            P(None, "tp"),
        ),
        out_specs=(P("seq", "tp"), P("seq", "tp", None), P("seq", "tp")),
        check_vma=False,
    )
```

```python
import functools
import jax
import jax.numpy as jnp
from jax import lax
from jax.experimental import pallas as pl
from jax.experimental.pallas import tpu as pltpu
from jax.sharding import PartitionSpec as P

LOG2E = 1.4426950408889634
NEG_FILL = -1e30
RESET = 1e30
YN = 4
ZN = 16
SEQ = YN * ZN
TPN = 8
WIN = 8
TOK = 128
ROWS = 256
PLANE = YN * TOK
GROUP = 16
MESH = pl.DeviceIdType.MESH
F32 = jnp.float32
BF16 = jnp.bfloat16


def starts_of(len_ref):
    s1 = len_ref[0]
    s2 = s1 + len_ref[1]
    s3 = s2 + len_ref[2]
    return (jnp.int32(0), s1, s2, s3)


def log1p_exp(v):
    return jnp.maximum(v, 0.0) + jnp.log1p(jnp.exp(-jnp.abs(v)))


def fill_group(g, base, starts, dt_ref, x_ref, bias, step_s, u_s):
    rows = pl.ds(pl.multiple_of(g * GROUP, GROUP), GROUP)
    raw = dt_ref[rows, :].astype(F32)
    x = x_ref[rows, :].astype(F32)
    step = log1p_exp(raw + bias)
    pos = base + g * GROUP + lax.broadcasted_iota(jnp.int32, (GROUP, 1), 0)
    hit = (pos == starts[0]) | (pos == starts[1]) | (pos == starts[2]) | (pos == starts[3])
    u_s[pl.ds(g * GROUP, GROUP)] = (step * x).reshape(GROUP, 16, 128)
    step_s[...] = (step + jnp.where(hit, RESET, 0.0)).reshape(GROUP, 16, 128)


def main_kernel(
    len_ref, k_ref, v_ref, x_ref, w_ref, dt_ref, bias_ref, alog_ref, skip_ref, q_ref,
    ctx_ref, out_ref,
    win_ref, parts, bc_v, bc_s, rate_s, step_s, u_s, fac_s, msg, ych, zout, zin, outb, inc_s, y_s, start_s, m_s, l_s, acc_s, qt_s, vt_s,
    own_sem, bc_sem, zs, zr, rs, rr, ls, lr, ks, kr, vs, vr, bs, br, ps, pr, qs, qr, fs, fr,
):
    seq = lax.axis_index("seq")
    tp = lax.axis_index("tp")
    z = seq // YN
    y = lax.rem(seq, YN)
    left_y = lax.rem(y + YN - 1, YN)
    right_y = lax.rem(y + 1, YN)

    def zy(dz, dy):
        return lax.rem(z + dz, ZN) * YN + lax.rem(y + dy, YN)

    up = zy(1, 0)
    right = zy(0, 1)
    left = zy(0, YN - 1)

    barrier = pltpu.get_barrier_semaphore()
    for dz in (1, 2, 4, ZN - 1, ZN - 2, ZN - 4):
        pl.semaphore_signal(barrier, inc=1, device_id=(zy(dz, 0), tp), device_id_type=MESH)
    for dy in range(1, YN):
        pl.semaphore_signal(barrier, inc=1, device_id=(zy(0, dy), tp), device_id_type=MESH)
    for off in range(1, TPN):
        pl.semaphore_signal(barrier, inc=1, device_id=(seq, lax.rem(tp + off, TPN)), device_id_type=MESH)
    pl.semaphore_wait(barrier, 6 + YN - 1 + TPN - 1)

    def remote(src, dst, ssem, rsem, peer):
        return pltpu.make_async_remote_copy(
            src_ref=src, dst_ref=dst, send_sem=ssem, recv_sem=rsem, device_id=(peer, tp), device_id_type=MESH
        )

    def block(s, h):
        return (k_ref, v_ref)[h] if s == 0 else win_ref.at[s, y, h]

    def z_copy(s, h):
        return remote(block(s - 1, h), win_ref.at[s, y, h], zs.at[h, s], zr.at[h, s], up)

    def right_copy(s, h):
        return remote(block(s, h), win_ref.at[s, y, h], rs.at[h, s], rr.at[h, s], right)

    def left_copy(s, h):
        return remote(block(s, h), win_ref.at[s, y, h], ls.at[h, s], lr.at[h, s], left)

    def k_copy(s):
        return remote(win_ref.at[s, left_y, 0], win_ref.at[s, left_y, 0], ks.at[s], kr.at[s], right)

    def v_copy(s):
        return remote(win_ref.at[s, right_y, 1], win_ref.at[s, right_y, 1], vs.at[s], vr.at[s], left)

    def spread(s):
        right_copy(s - 1, 0).wait_recv()
        k_copy(s - 1).start()
        left_copy(s - 1, 1).wait_recv()
        v_copy(s - 1).start()

    def kv_step(s):
        for h in (0, 1):
            z_copy(s, h).wait_recv()
            if s < WIN:
                z_copy(s + 1, h).start()
            right_copy(s, h).start()
            left_copy(s, h).start()
        spread(s)

    own = [pltpu.make_async_copy((k_ref, v_ref)[h], win_ref.at[0, y, h], own_sem.at[h]) for h in (0, 1)]
    for h in (0, 1):
        z_copy(1, h).start()
    for h in (0, 1):
        right_copy(0, h).start()
        left_copy(0, h).start()
        own[h].start()

    parts[tp] = lax.dot_general(w_ref[...], x_ref[...], (((1,), (1,)), ((), ())), preferred_element_type=F32)

    def bc_copy(off):
        return pltpu.make_async_remote_copy(
            src_ref=parts.at[tp], dst_ref=parts.at[tp], send_sem=bs.at[off], recv_sem=br.at[off],
            device_id=(seq, lax.rem(tp + off, TPN)), device_id_type=MESH,
        )

    for off in range(1, TPN):
        bc_copy(off).start()

    rate_s[...] = (jnp.exp(alog_ref[...]) * (-LOG2E)).reshape(16, 16, 128)
    msg[...] = jnp.zeros_like(msg)
    bias = bias_ref[...]
    base = seq * TOK
    starts = starts_of(len_ref)
    scale = LOG2E / 128.0**0.5

    def ready(dz):
        right_copy(dz, 1).wait_recv()
        left_copy(dz, 0).wait_recv()
        k_copy(dz).wait_recv()
        v_copy(dz).wait_recv()

    def attend_plane(dz):
        ready(dz)

        @pl.when(z >= dz)
        def _():
            vt_s[...] = win_ref[dz, :, 1].reshape(PLANE, 128).astype(F32).T.astype(BF16)

            @pl.loop(0, 1024 // ROWS)
            def _(rt):
                cols = pl.ds(pl.multiple_of(rt * ROWS, ROWS), ROWS)
                kk = win_ref[dz, :, 0].reshape(PLANE, 128)
                key_pos = lax.broadcasted_iota(jnp.int32, (PLANE, ROWS), 0)
                first = start_s[:, cols] - (z - dz) * PLANE
                sc = jnp.dot(kk, qt_s[:, cols], preferred_element_type=F32)
                ok = key_pos >= first
                if dz == 0:
                    last = y * TOK + rt * (ROWS // 8) + lax.broadcasted_iota(jnp.int32, (1, ROWS), 1) // 8
                    ok = ok & (key_pos <= last)
                sc = jnp.where(ok, sc, NEG_FILL)
                top = jnp.max(sc, axis=0, keepdims=True)
                if dz > 0:
                    old = m_s[:, cols]
                    top = jnp.maximum(old, top)
                e = jnp.exp2((sc - top) * scale)
                total = jnp.sum(e, axis=0, keepdims=True)
                prod = jnp.dot(vt_s[...], e.astype(BF16), preferred_element_type=F32)
                if dz > 0:
                    fix = jnp.exp2((old - top) * scale)
                    total = l_s[:, cols] * fix + total
                    prod = acc_s[:, cols] * fix + prod
                m_s[:, cols] = top
                l_s[:, cols] = total
                acc_s[:, cols] = prod

    qpos = base + lax.broadcasted_iota(jnp.int32, (1, 1024), 1) // 8
    qstart = jnp.zeros((1, 1024), jnp.int32)
    for r in range(1, 4):
        qstart = jnp.where(qpos >= starts[r], starts[r], qstart)
    start_s[...] = qstart
    qt_s[...] = q_ref[...].astype(F32).T.astype(BF16)

    kv_step(1)
    for off in range(1, TPN):
        bc_copy(off).wait_recv()
    total_bc = parts[0]
    for t in range(1, TPN):
        total_bc = total_bc + parts[t]
    bc_v[...] = total_bc
    to_smem = pltpu.make_async_copy(bc_v, bc_s, bc_sem)
    to_smem.start()
    to_smem.wait()

    def scan_groups(lo, hi):
        @pl.loop(lo, hi)
        def _(g):
            fill_group(g, base, starts, dt_ref, x_ref, bias, step_s, u_s)

            def token(t, carry):
                states, total = carry
                st = step_s[t]
                p = g * GROUP + t
                u = u_s[p]
                new = []
                for n in range(16):
                    f = jnp.exp2(st * rate_s[n])
                    fac_s[p, n] = f
                    new.append(f * states[n] + u * bc_s[n, p])
                return tuple(new), total + st

            init = (tuple(msg[n // 4, n % 4] for n in range(16)), msg[0, 4])
            states, total = lax.fori_loop(0, GROUP, token, init, unroll=4)
            for n in range(16):
                msg[n // 4, n % 4] = states[n]
            msg[0, 4] = total

    scan_groups(0, 3)
    kv_step(2)
    scan_groups(3, 6)
    kv_step(3)
    scan_groups(6, 8)
    total = msg[0, 4]
    for q in range(1, 4):
        msg[q, 4] = total

    def part_copy(d):
        return remote(msg.at[lax.rem(y + d, YN)], ych.at[y], ps.at[d], pr.at[d], zy(0, d))

    for d in (1, 3, 2):
        part_copy(d).start()
    ych[y] = msg[y]
    kv_step(4)
    for h in (0, 1):
        own[h].wait()
    attend_plane(0)
    attend_plane(1)
    for d in range(1, YN):
        part_copy(d).wait_recv()
    rate = rate_s[pl.ds(4 * y, 4)]
    acc = ych[0, 0:4]
    dec = ych[0, 4]
    for c in range(1, YN):
        acc = jnp.exp2(rate * ych[c, 4][None]) * acc + ych[c, 0:4]
        dec = dec + ych[c, 4]

    def z_round(j, d):
        return remote(zout.at[j], zin.at[j], qs.at[j], qr.at[j], zy(d, 0))

    for j, d in enumerate((1, 1, 2, 4)):
        zout[j, 0:4] = acc
        zout[j, 4] = dec
        z_round(j, d).start()
        kv_step(5 + j)
        for dz in ((), (2,), (3, 4), (5, 6))[j]:
            attend_plane(dz)
        if j == 3:
            spread(WIN + 1)
            attend_plane(7)
        z_round(j, d).wait_recv()
        here = (z >= d).astype(F32)
        got = zin[j, 0:4] * here
        got_dec = zin[j, 4] * here
        if j == 0:
            acc, dec = got, got_dec
        else:
            acc = acc + jnp.exp2(rate * dec[None]) * got
            dec = dec + got_dec

    for c in range(YN):
        outb[c] = acc
        if c < YN - 1:
            acc = jnp.exp2(rate * ych[c, 4][None]) * acc + ych[c, 0:4]

    def back_copy(d):
        return remote(outb.at[lax.rem(y + d, YN)], inc_s.at[y], fs.at[d], fr.at[d], zy(0, d))

    for d in (1, 3, 2):
        back_copy(d).start()
    inc_s[y] = outb[y]
    attend_plane(8)
    ctx_ref[...] = (acc_s[...] / l_s[...]).T.astype(BF16)
    for d in range(1, YN):
        back_copy(d).wait_recv()
    skip = skip_ref[...]

    @pl.loop(0, TOK // GROUP)
    def _(g):
        def token(t, states):
            p = g * GROUP + t
            u = u_s[p]
            new = []
            total = None
            for n in range(16):
                state = fac_s[p, n] * states[n] + u * bc_s[n, p]
                new.append(state)
                term = state * bc_s[16 + n, p]
                total = term if total is None else total + term
            y_s[t] = total
            return tuple(new)

        states = lax.fori_loop(0, GROUP, token, tuple(inc_s[n // 4, n % 4] for n in range(16)), unroll=4)
        for n in range(16):
            inc_s[n // 4, n % 4] = states[n]
        rows = pl.ds(pl.multiple_of(g * GROUP, GROUP), GROUP)
        x = x_ref[rows, :].astype(F32)
        out_ref[rows, :] = (y_s[...].reshape(GROUP, 2048) + skip * x).astype(BF16)

    for off in range(1, TPN):
        bc_copy(off).wait_send()
    for d in range(1, YN):
        part_copy(d).wait_send()
        back_copy(d).wait_send()
    for j, d in enumerate((1, 1, 2, 4)):
        z_round(j, d).wait_send()
    for s in range(WIN + 1):
        for h in (0, 1):
            if s > 0:
                z_copy(s, h).wait_send()
            right_copy(s, h).wait_send()
            left_copy(s, h).wait_send()
        k_copy(s).wait_send()
        v_copy(s).wait_send()


def main_pass(*args):
    vm = pl.BlockSpec(memory_space=pltpu.VMEM)
    sm = pl.BlockSpec(memory_space=pltpu.SMEM)
    dma = pltpu.SemaphoreType.DMA
    n = WIN + 1
    return pl.pallas_call(
        main_kernel,
        out_shape=(
            jax.ShapeDtypeStruct((1024, 128), BF16),
            jax.ShapeDtypeStruct((TOK, 2048), BF16),
        ),
        in_specs=[sm] + [vm] * 9,
        out_specs=(vm, vm),
        scratch_shapes=[
            pltpu.VMEM((n, YN, 2, TOK, 128), BF16),
            pltpu.VMEM((TPN, 32, TOK), F32),
            pltpu.VMEM((32, TOK), F32),
            pltpu.SMEM((32, TOK), F32),
            pltpu.VMEM((16, 16, 128), F32),
            pltpu.VMEM((GROUP, 16, 128), F32),
            pltpu.VMEM((TOK, 16, 128), F32),
            pltpu.VMEM((TOK, 16, 16, 128), F32),
            pltpu.VMEM((YN, 5, 16, 128), F32),
            pltpu.VMEM((YN, 5, 16, 128), F32),
            pltpu.VMEM((4, 5, 16, 128), F32),
            pltpu.VMEM((4, 5, 16, 128), F32),
            pltpu.VMEM((YN, 4, 16, 128), F32),
            pltpu.VMEM((YN, 4, 16, 128), F32),
            pltpu.VMEM((GROUP, 16, 128), F32),
            pltpu.VMEM((1, 1024), jnp.int32),
            pltpu.VMEM((1, 1024), F32),
            pltpu.VMEM((1, 1024), F32),
            pltpu.VMEM((128, 1024), F32),
            pltpu.VMEM((128, 1024), BF16),
            pltpu.VMEM((128, PLANE), BF16),
            dma((2,)),
            dma(()),
        ]
        + [dma((2, n)) for _ in range(6)]
        + [dma((n,)) for _ in range(4)]
        + [dma((TPN,)), dma((TPN,))]
        + [dma((4,)) for _ in range(6)],
        compiler_params=pltpu.CompilerParams(collective_id=0, has_side_effects=True),
        name="layer",
    )(*args)


def finish_kernel(len_ref, idx_ref, num_ref, ctx_ref, mix_ref, res_ref, table_ref, ctx_out, mix_out, st_out):
    base = lax.axis_index("seq") * TOK
    starts = starts_of(len_ref)
    ctx_out[...] = ctx_ref[...]
    mix_out[...] = mix_ref[...]
    table = table_ref[...].astype(F32)
    tpos = base + lax.broadcasted_iota(jnp.int32, (TOK, 1), 0)
    add = jnp.zeros((TOK, 1024), F32)
    for r in range(4):
        vec = jnp.zeros((1, 1024), F32)
        for i in range(7):
            vec = jnp.where(idx_ref[r] == i, table[i : i + 1], vec)
        add = jnp.where(tpos >= starts[r], vec * (num_ref[r].astype(F32) * 0.25), add)
    st_out[...] = (res_ref[...].astype(F32) + add).astype(BF16)


def finish(lengths, index, num, ctx, mixed, residual, table):
    vm = pl.BlockSpec(memory_space=pltpu.VMEM)
    sm = pl.BlockSpec(memory_space=pltpu.SMEM)
    return pl.pallas_call(
        finish_kernel,
        out_shape=tuple(jax.ShapeDtypeStruct(v.shape, BF16) for v in (ctx, mixed, residual)),
        in_specs=[sm] * 3 + [vm] * 4,
        out_specs=(vm, vm, vm),
        name="steer_finish",
    )(lengths, index, num, ctx, mixed, residual, table)


def shards(residual, steer_table, steer_index, steer_num, lengths, queries, keys, values, inner_x, dt_raw, dt_bias, a_log, skip_gain, bc_weight):
    ctx, mixed = main_pass(
        lengths,
        keys.reshape(TOK, 128),
        values.reshape(TOK, 128),
        inner_x,
        bc_weight,
        dt_raw,
        dt_bias[None, :],
        a_log,
        skip_gain[None, :],
        queries.reshape(1024, 128),
    )
    ctx, mixed, steered = finish(lengths, steer_index, steer_num, ctx, mixed, residual, steer_table)
    return steered, ctx.reshape(queries.shape), mixed


def solution(mesh):
    return jax.shard_map(
        shards,
        mesh=mesh,
        in_specs=(
            P("seq", "tp"),
            P(None, "tp"),
            P(),
            P(),
            P(),
            P("seq", "tp", None),
            P("seq", "tp", None),
            P("seq", "tp", None),
            P("seq", "tp"),
            P("seq", "tp"),
            P("tp"),
            P(None, "tp"),
            P("tp"),
            P(None, "tp"),
        ),
        out_specs=(P("seq", "tp"), P("seq", "tp", None), P("seq", "tp")),
        check_vma=False,
    )
```

```python
import functools
import jax
import jax.numpy as jnp
from jax import lax
from jax.experimental import pallas as pl
from jax.experimental.pallas import tpu as pltpu
from jax.sharding import PartitionSpec as P

LOG2E = 1.4426950408889634
NEG_FILL = -1e30
RESET = 1e30
YN = 4
ZN = 16
SEQ = YN * ZN
TPN = 8
WIN = 8
TOK = 128
ROWS = 256
PLANE = YN * TOK
GROUP = 16
MESH = pl.DeviceIdType.MESH
F32 = jnp.float32
BF16 = jnp.bfloat16


def starts_of(len_ref):
    s1 = len_ref[0]
    s2 = s1 + len_ref[1]
    s3 = s2 + len_ref[2]
    return (jnp.int32(0), s1, s2, s3)


def log1p_exp(v):
    return jnp.maximum(v, 0.0) + jnp.log1p(jnp.exp(-jnp.abs(v)))


def fill_group(g, base, starts, dt_ref, x_ref, bias, step_s, u_s):
    rows = pl.ds(pl.multiple_of(g * GROUP, GROUP), GROUP)
    raw = dt_ref[rows, :].astype(F32)
    x = x_ref[rows, :].astype(F32)
    step = log1p_exp(raw + bias)
    pos = base + g * GROUP + lax.broadcasted_iota(jnp.int32, (GROUP, 1), 0)
    hit = (pos == starts[0]) | (pos == starts[1]) | (pos == starts[2]) | (pos == starts[3])
    u_s[pl.ds(g * GROUP, GROUP)] = (step * x).reshape(GROUP, 16, 128)
    step_s[pl.ds(g * GROUP, GROUP)] = (step + jnp.where(hit, RESET, 0.0)).reshape(GROUP, 16, 128)


def main_kernel(
    len_ref, k_ref, v_ref, x_ref, w_ref, dt_ref, bias_ref, alog_ref, skip_ref, q_ref,
    ctx_ref, out_ref,
    win_ref, parts, bc_v, bc_s, rate_s, step_s, u_s, fac_s, msg, ych, zout, zin, outb, inc_s, y_s, start_s, m_s, l_s, acc_s, qt_s, vt_s, far_out, far_in,
    own_sem, bc_sem, zs, zr, rs, rr, ls, lr, ks, kr, vs, vr, bs, br, ps, pr, qs, qr, fs, fr,
):
    seq = lax.axis_index("seq")
    tp = lax.axis_index("tp")
    z = seq // YN
    y = lax.rem(seq, YN)
    left_y = lax.rem(y + YN - 1, YN)
    right_y = lax.rem(y + 1, YN)

    def zy(dz, dy):
        return lax.rem(z + dz, ZN) * YN + lax.rem(y + dy, YN)

    up = zy(1, 0)
    right = zy(0, 1)
    left = zy(0, YN - 1)

    barrier = pltpu.get_barrier_semaphore()
    for dz in (1, 2, 4, ZN - 1, ZN - 2, ZN - 4):
        pl.semaphore_signal(barrier, inc=1, device_id=(zy(dz, 0), tp), device_id_type=MESH)
    for dy in range(1, YN):
        pl.semaphore_signal(barrier, inc=1, device_id=(zy(0, dy), tp), device_id_type=MESH)
    for off in range(1, TPN):
        pl.semaphore_signal(barrier, inc=1, device_id=(seq, lax.rem(tp + off, TPN)), device_id_type=MESH)
    pl.semaphore_wait(barrier, 6 + YN - 1 + TPN - 1)

    def remote(src, dst, ssem, rsem, peer):
        return pltpu.make_async_remote_copy(
            src_ref=src, dst_ref=dst, send_sem=ssem, recv_sem=rsem, device_id=(peer, tp), device_id_type=MESH
        )

    def block(s, h):
        return (k_ref, v_ref)[h] if s == 0 else win_ref.at[s, y, h]

    def z_copy(s, h):
        return remote(block(s - 1, h), win_ref.at[s, y, h], zs.at[h, s], zr.at[h, s], up)

    def right_copy(s, h):
        return remote(block(s, h), win_ref.at[s, y, h], rs.at[h, s], rr.at[h, s], right)

    def left_copy(s, h):
        return remote(block(s, h), win_ref.at[s, y, h], ls.at[h, s], lr.at[h, s], left)

    def k_copy(s):
        return remote(win_ref.at[s, left_y, 0], win_ref.at[s, left_y, 0], ks.at[s], kr.at[s], right)

    def v_copy(s):
        return remote(win_ref.at[s, right_y, 1], win_ref.at[s, right_y, 1], vs.at[s], vr.at[s], left)

    def spread(s):
        right_copy(s - 1, 0).wait_recv()
        k_copy(s - 1).start()
        left_copy(s - 1, 1).wait_recv()
        v_copy(s - 1).start()

    def kv_step(s):
        for h in (0, 1):
            z_copy(s, h).wait_recv()
            if s < WIN:
                z_copy(s + 1, h).start()
            right_copy(s, h).start()
            left_copy(s, h).start()
        spread(s)

    own = [pltpu.make_async_copy((k_ref, v_ref)[h], win_ref.at[0, y, h], own_sem.at[h]) for h in (0, 1)]
    for h in (0, 1):
        z_copy(1, h).start()
    for h in (0, 1):
        right_copy(0, h).start()
        left_copy(0, h).start()
        own[h].start()

    parts[tp] = lax.dot_general(w_ref[...], x_ref[...], (((1,), (1,)), ((), ())), preferred_element_type=F32)

    def bc_copy(off):
        return pltpu.make_async_remote_copy(
            src_ref=parts.at[tp], dst_ref=parts.at[tp], send_sem=bs.at[off], recv_sem=br.at[off],
            device_id=(seq, lax.rem(tp + off, TPN)), device_id_type=MESH,
        )

    for off in range(1, TPN):
        bc_copy(off).start()

    rate_s[...] = (jnp.exp(alog_ref[...]) * (-LOG2E)).reshape(16, 16, 128)
    msg[...] = jnp.zeros_like(msg)
    bias = bias_ref[...]
    base = seq * TOK
    starts = starts_of(len_ref)
    scale = LOG2E / 128.0**0.5

    def ready(dz):
        right_copy(dz, 1).wait_recv()
        left_copy(dz, 0).wait_recv()
        k_copy(dz).wait_recv()
        v_copy(dz).wait_recv()

    def attend_plane(dz):
        ready(dz)

        @pl.when(z >= dz)
        def _():
            vt_s[...] = win_ref[dz, :, 1].reshape(PLANE, 128).astype(F32).T.astype(BF16)

            @pl.loop(0, 1024 // ROWS)
            def _(rt):
                cols = pl.ds(pl.multiple_of(rt * ROWS, ROWS), ROWS)
                kk = win_ref[dz, :, 0].reshape(PLANE, 128)
                key_pos = lax.broadcasted_iota(jnp.int32, (PLANE, ROWS), 0)
                first = start_s[:, cols] - (z - dz) * PLANE
                sc = jnp.dot(kk, qt_s[:, cols], preferred_element_type=F32)
                ok = key_pos >= first
                if dz == 0:
                    last = y * TOK + rt * (ROWS // 8) + lax.broadcasted_iota(jnp.int32, (1, ROWS), 1) // 8
                    ok = ok & (key_pos <= last)
                sc = jnp.where(ok, sc, NEG_FILL)
                top = jnp.max(sc, axis=0, keepdims=True)
                if dz > 0:
                    old = m_s[:, cols]
                    top = jnp.maximum(old, top)
                e = jnp.exp2((sc - top) * scale)
                total = jnp.sum(e, axis=0, keepdims=True)
                prod = jnp.dot(vt_s[...], e.astype(BF16), preferred_element_type=F32)
                if dz > 0:
                    fix = jnp.exp2((old - top) * scale)
                    total = l_s[:, cols] * fix + total
                    prod = acc_s[:, cols] * fix + prod
                m_s[:, cols] = top
                l_s[:, cols] = total
                acc_s[:, cols] = prod

    qpos = base + lax.broadcasted_iota(jnp.int32, (1, 1024), 1) // 8
    qstart = jnp.zeros((1, 1024), jnp.int32)
    for r in range(1, 4):
        qstart = jnp.where(qpos >= starts[r], starts[r], qstart)
    start_s[...] = qstart
    qt_s[...] = q_ref[...].astype(F32).T.astype(BF16)

    def factors(p, c):
        st = step_s[p]
        for n in range(16):
            fac_s[p, n] = jnp.exp2(st * rate_s[n])
        return c

    def prepare(lo, hi):
        @pl.loop(lo, hi)
        def _(g):
            fill_group(g, base, starts, dt_ref, x_ref, bias, step_s, u_s)
            lax.fori_loop(g * GROUP, g * GROUP + GROUP, factors, 0)

    prepare(0, 5)
    kv_step(1)
    prepare(5, 8)
    for off in range(1, TPN):
        bc_copy(off).wait_recv()
    total_bc = parts[0]
    for t in range(1, TPN):
        total_bc = total_bc + parts[t]
    bc_v[...] = total_bc
    to_smem = pltpu.make_async_copy(bc_v, bc_s, bc_sem)
    to_smem.start()
    to_smem.wait()

    def scan_groups(lo, hi):
        @pl.loop(lo, hi)
        def _(g):
            def token(t, carry):
                states, total = carry
                p = g * GROUP + t
                st = step_s[p]
                u = u_s[p]
                new = []
                for n in range(16):
                    new.append(fac_s[p, n] * states[n] + u * bc_s[n, p])
                return tuple(new), total + st

            init = (tuple(msg[n // 4, n % 4] for n in range(16)), msg[0, 4])
            states, total = lax.fori_loop(0, GROUP, token, init, unroll=4)
            for n in range(16):
                msg[n // 4, n % 4] = states[n]
            msg[0, 4] = total

    scan_groups(0, 3)
    kv_step(2)
    scan_groups(3, 6)
    kv_step(3)
    scan_groups(6, 8)
    total = msg[0, 4]
    for q in range(1, 4):
        msg[q, 4] = total

    def part_copy(d):
        return remote(msg.at[lax.rem(y + d, YN)], ych.at[y], ps.at[d], pr.at[d], zy(0, d))

    for d in (1, 3, 2):
        part_copy(d).start()
    ych[y] = msg[y]
    kv_step(4)
    for h in (0, 1):
        own[h].wait()
    attend_plane(0)
    attend_plane(1)
    for d in range(1, YN):
        part_copy(d).wait_recv()
    rate = rate_s[pl.ds(4 * y, 4)]
    acc = ych[0, 0:4]
    dec = ych[0, 4]
    for c in range(1, YN):
        acc = jnp.exp2(rate * ych[c, 4][None]) * acc + ych[c, 0:4]
        dec = dec + ych[c, 4]

    def z_round(j, d):
        if j == 3:
            return remote(far_out, far_in, qs.at[j], qr.at[j], zy(d, 0))
        return remote(zout.at[j], zin.at[j], qs.at[j], qr.at[j], zy(d, 0))

    for j, d in enumerate((1, 1, 2, 4)):
        if j == 3:
            far_out[...] = acc.astype(BF16)
        else:
            zout[j, 0:4] = acc
            zout[j, 4] = dec
        z_round(j, d).start()
        kv_step(5 + j)
        for dz in ((), (2,), (3, 4), (5, 6))[j]:
            attend_plane(dz)
        if j == 3:
            spread(WIN + 1)
            attend_plane(7)
        z_round(j, d).wait_recv()
        here = (z >= d).astype(F32)
        if j == 3:
            acc = acc + jnp.exp2(rate * dec[None]) * (far_in[...].astype(F32) * here)
            continue
        got = zin[j, 0:4] * here
        got_dec = zin[j, 4] * here
        if j == 0:
            acc, dec = got, got_dec
        else:
            acc = acc + jnp.exp2(rate * dec[None]) * got
            dec = dec + got_dec

    for c in range(YN):
        outb[c] = acc
        if c < YN - 1:
            acc = jnp.exp2(rate * ych[c, 4][None]) * acc + ych[c, 0:4]

    def back_copy(d):
        return remote(outb.at[lax.rem(y + d, YN)], inc_s.at[y], fs.at[d], fr.at[d], zy(0, d))

    for d in (1, 3, 2):
        back_copy(d).start()
    inc_s[y] = outb[y]
    attend_plane(8)
    ctx_ref[...] = (acc_s[...] / l_s[...]).T.astype(BF16)
    for d in range(1, YN):
        back_copy(d).wait_recv()
    skip = skip_ref[...]

    @pl.loop(0, TOK // GROUP)
    def _(g):
        def token(t, states):
            p = g * GROUP + t
            u = u_s[p]
            new = []
            total = None
            for n in range(16):
                state = fac_s[p, n] * states[n] + u * bc_s[n, p]
                new.append(state)
                term = state * bc_s[16 + n, p]
                total = term if total is None else total + term
            y_s[t] = total
            return tuple(new)

        states = lax.fori_loop(0, GROUP, token, tuple(inc_s[n // 4, n % 4] for n in range(16)), unroll=4)
        for n in range(16):
            inc_s[n // 4, n % 4] = states[n]
        rows = pl.ds(pl.multiple_of(g * GROUP, GROUP), GROUP)
        x = x_ref[rows, :].astype(F32)
        out_ref[rows, :] = (y_s[...].reshape(GROUP, 2048) + skip * x).astype(BF16)

    for off in range(1, TPN):
        bc_copy(off).wait_send()
    for d in range(1, YN):
        part_copy(d).wait_send()
        back_copy(d).wait_send()
    for j, d in enumerate((1, 1, 2, 4)):
        z_round(j, d).wait_send()
    for s in range(WIN + 1):
        for h in (0, 1):
            if s > 0:
                z_copy(s, h).wait_send()
            right_copy(s, h).wait_send()
            left_copy(s, h).wait_send()
        k_copy(s).wait_send()
        v_copy(s).wait_send()


def main_pass(*args):
    vm = pl.BlockSpec(memory_space=pltpu.VMEM)
    sm = pl.BlockSpec(memory_space=pltpu.SMEM)
    dma = pltpu.SemaphoreType.DMA
    n = WIN + 1
    return pl.pallas_call(
        main_kernel,
        out_shape=(
            jax.ShapeDtypeStruct((1024, 128), BF16),
            jax.ShapeDtypeStruct((TOK, 2048), BF16),
        ),
        in_specs=[sm] + [vm] * 9,
        out_specs=(vm, vm),
        scratch_shapes=[
            pltpu.VMEM((n, YN, 2, TOK, 128), BF16),
            pltpu.VMEM((TPN, 32, TOK), F32),
            pltpu.VMEM((32, TOK), F32),
            pltpu.SMEM((32, TOK), F32),
            pltpu.VMEM((16, 16, 128), F32),
            pltpu.VMEM((TOK, 16, 128), F32),
            pltpu.VMEM((TOK, 16, 128), F32),
            pltpu.VMEM((TOK, 16, 16, 128), F32),
            pltpu.VMEM((YN, 5, 16, 128), F32),
            pltpu.VMEM((YN, 5, 16, 128), F32),
            pltpu.VMEM((3, 5, 16, 128), F32),
            pltpu.VMEM((3, 5, 16, 128), F32),
            pltpu.VMEM((YN, 4, 16, 128), F32),
            pltpu.VMEM((YN, 4, 16, 128), F32),
            pltpu.VMEM((GROUP, 16, 128), F32),
            pltpu.VMEM((1, 1024), jnp.int32),
            pltpu.VMEM((1, 1024), F32),
            pltpu.VMEM((1, 1024), F32),
            pltpu.VMEM((128, 1024), F32),
            pltpu.VMEM((128, 1024), BF16),
            pltpu.VMEM((128, PLANE), BF16),
            pltpu.VMEM((4, 16, 128), BF16),
            pltpu.VMEM((4, 16, 128), BF16),
            dma((2,)),
            dma(()),
        ]
        + [dma((2, n)) for _ in range(6)]
        + [dma((n,)) for _ in range(4)]
        + [dma((TPN,)), dma((TPN,))]
        + [dma((4,)) for _ in range(6)],
        compiler_params=pltpu.CompilerParams(collective_id=0, has_side_effects=True),
        name="layer",
    )(*args)


def finish_kernel(len_ref, idx_ref, num_ref, ctx_ref, mix_ref, res_ref, table_ref, ctx_out, mix_out, st_out):
    base = lax.axis_index("seq") * TOK
    starts = starts_of(len_ref)
    ctx_out[...] = ctx_ref[...]
    mix_out[...] = mix_ref[...]
    table = table_ref[...].astype(F32)
    tpos = base + lax.broadcasted_iota(jnp.int32, (TOK, 1), 0)
    add = jnp.zeros((TOK, 1024), F32)
    for r in range(4):
        vec = jnp.zeros((1, 1024), F32)
        for i in range(7):
            vec = jnp.where(idx_ref[r] == i, table[i : i + 1], vec)
        add = jnp.where(tpos >= starts[r], vec * (num_ref[r].astype(F32) * 0.25), add)
    st_out[...] = (res_ref[...].astype(F32) + add).astype(BF16)


def finish(lengths, index, num, ctx, mixed, residual, table):
    vm = pl.BlockSpec(memory_space=pltpu.VMEM)
    sm = pl.BlockSpec(memory_space=pltpu.SMEM)
    return pl.pallas_call(
        finish_kernel,
        out_shape=tuple(jax.ShapeDtypeStruct(v.shape, BF16) for v in (ctx, mixed, residual)),
        in_specs=[sm] * 3 + [vm] * 4,
        out_specs=(vm, vm, vm),
        name="steer_finish",
    )(lengths, index, num, ctx, mixed, residual, table)


def shards(residual, steer_table, steer_index, steer_num, lengths, queries, keys, values, inner_x, dt_raw, dt_bias, a_log, skip_gain, bc_weight):
    ctx, mixed = main_pass(
        lengths,
        keys.reshape(TOK, 128),
        values.reshape(TOK, 128),
        inner_x,
        bc_weight,
        dt_raw,
        dt_bias[None, :],
        a_log,
        skip_gain[None, :],
        queries.reshape(1024, 128),
    )
    ctx, mixed, steered = finish(lengths, steer_index, steer_num, ctx, mixed, residual, steer_table)
    return steered, ctx.reshape(queries.shape), mixed


def solution(mesh):
    return jax.shard_map(
        shards,
        mesh=mesh,
        in_specs=(
            P("seq", "tp"),
            P(None, "tp"),
            P(),
            P(),
            P(),
            P("seq", "tp", None),
            P("seq", "tp", None),
            P("seq", "tp", None),
            P("seq", "tp"),
            P("seq", "tp"),
            P("tp"),
            P(None, "tp"),
            P("tp"),
            P(None, "tp"),
        ),
        out_specs=(P("seq", "tp"), P("seq", "tp", None), P("seq", "tp")),
        check_vma=False,
    )
```
